32 devices in a mesh: tile: 4 (over z), text: 8 (over y, x, core).
Axes of the slice: x: 2, y: 2, z: 4, core: 2. Of those that a mesh axis runs over, the one named last changes fastest.
Arguments:
- grad_seq: bfloat16 [2560, 8192], P('text', 'tile'), may hold values from -6 to 6
- positions: int32 [2560], replicated, may hold values from 0 to 2559, each once
- pre_act: bfloat16 [2560, 5120], P('tile', 'text'), may hold values from -6 to 6
- w_out: bfloat16 [5120, 8192], P('text', 'tile'), may hold values from -0.078125 to 0.078125
Outputs:
- grad_pre: float32 [2560, 5120], P('tile', 'text')
- grad_w_out: float32 [5120, 8192], P('text', 'tile')
- grad_bias: float32 [8192], P('tile')
The draws below stay inside these ranges and needn't reach their ends.
Inputs may be any that keep to these rules, and one draw needn't show every extreme that they name: positions names every place 0 to 2559 once.
All inputs are finite; a program needn't handle non-finite values.
Results may differ from the reference program's by a relative error of at most 0.003.
Values may be sent and summed in bfloat16 or wider, within the bound.
A program may use at most 128 MiB of HBM per device.

```python
import jax
import jax.numpy as jnp
from jax import lax

DM = 5120
OUT = 8192
SLOTS = 2560
N_TILE = 4


def spiked(array, rng, source, target, blocks, factor):
    owner, partner = [(jnp.arange(array.shape[position]) // (array.shape[position] // blocks)).reshape([-1 if axis == position else 1 for axis in range(array.ndim)]) for position in (source, target)]
    chosen = jax.random.permutation(rng, blocks)[partner]
    strong = (owner == chosen) | (owner == (partner + blocks // 2) % blocks)
    return jnp.where(strong, factor * array, array)


def steps_of(rng, dims, pieces, least, high):
    loudness = 1.0
    for dim, parts in pieces:
        draws = jax.random.uniform(jax.random.fold_in(jax.random.fold_in(rng, 6), dim), (parts,), jnp.float32, least / len(pieces), high / len(pieces))
        loudness = loudness * jnp.repeat(jnp.exp(draws), dims[dim] // parts).reshape((-1,) + (1,) * (len(dims) - 1 - dim))
    return loudness


def normal_values(key, extent, scale, bound, cuts=(), kind=jnp.bfloat16):
    loudness = steps_of(key, extent, cuts, -0.22, 0.18) if cuts else 1.0
    array = jax.random.normal(key, extent, jnp.float32) * scale * loudness
    return jnp.minimum(jnp.maximum(array, -bound), bound).astype(kind)


def noise_with(key, extent, scale, reach, cuts, heavy, held_as=jnp.bfloat16):
    drawn = scale * jax.random.normal(key, extent, jnp.float32)
    if cuts:
        drawn = drawn * steps_of(key, extent, cuts, -0.22, 0.18)
    return jnp.clip(spiked(drawn, jax.random.fold_in(key, 3), *heavy), -reach, reach).astype(held_as)


def setup_inputs(seed: int = 0) -> dict:
    key_list = jax.random.split(jax.random.key(seed), 5)
    return {
        "grad_seq": noise_with(key_list[0], (SLOTS, OUT), 1.0, 6.0, ((0, 8), (1, 4)), (0, 1, 8, 2.0)),
        "positions": jax.random.permutation(key_list[1], SLOTS).astype(jnp.int32),
        "pre_act": normal_values(key_list[2], (SLOTS, DM), 1.0, 6.0, ((0, 4), (1, 8))),
        "w_out": normal_values(key_list[3], (DM, OUT), DM ** -0.5, 0.078125, ((0, 8), (1, 4))),
    }


def gelu_parts(pre):
    value = pre.astype(jnp.float32)
    cdf = 0.5 * (1.0 + jax.scipy.special.erf(value * 0.7071067811865476))
    activated = value * cdf
    slope = cdf + value * jnp.exp(-0.5 * value * value) * 0.3989422804014327
    return activated, slope


def reference(grad_seq, positions, pre_act, w_out):
    slot_grad = jnp.take(grad_seq, positions.astype(jnp.int32), axis=0)
    activated, slope = gelu_parts(pre_act)
    act_bf = activated.astype(jnp.bfloat16)
    width = OUT // N_TILE

    def add_block(total, block_index):
        start = (block_index * width).astype(jnp.int32)
        grad_block = lax.dynamic_slice_in_dim(slot_grad, start, width, 1)
        weight_block = lax.dynamic_slice_in_dim(w_out, start, width, 1)
        partial_term = jnp.dot(grad_block, weight_block.T, preferred_element_type=jnp.float32)
        return total + partial_term, None

    start_total = jnp.zeros((slot_grad.shape[0], w_out.shape[0]), jnp.float32)
    grad_act, _ = lax.scan(add_block, start_total, jnp.arange(N_TILE, dtype=jnp.int32))
    grad_pre = grad_act * slope
    grad_w_out = jnp.dot(act_bf.T, slot_grad, preferred_element_type=jnp.float32)
    grad_bias = jnp.sum(grad_seq.astype(jnp.float32), axis=0)
    return grad_pre, grad_w_out, grad_bias
```

```python
import jax
import jax.numpy as jnp
from jax import lax
from jax.experimental import pallas as pl
from jax.experimental.pallas import tpu as pltpu
from jax.sharding import PartitionSpec as P


def gelu_parts(pre):
    value = pre.astype(jnp.float32)
    cdf = 0.5 * (1.0 + jax.scipy.special.erf(value * 0.7071067811865476))
    activated = value * cdf
    slope = cdf + value * jnp.exp(-0.5 * value * value) * 0.3989422804014327
    return (activated, slope)


def rows_of(table, index):
    return table.at[index].get(mode="promise_in_bounds", unique_indices=True)


def fused_kernel(n, subs, width, g_ref, w_ref, pre_ref, place_ref, grad_ref, weight_ref, bias_ref,
                 held, weight, term, pre, act, turned, own, spots, arrive, leave,
                 send_sem, recv_sem, act_send, act_recv, sum_send, sum_recv, own_sem):
    t, me = lax.axis_index("text"), lax.axis_index("tile")
    core, x, y = t % 2, t // 2 % 2, t // 4
    across, beside, above = 1 - 2 * core, 2 - 4 * x, 4 - 8 * y
    mate, xn, yn = t + across, t + beside, t + above
    diag = t + beside + above
    mesh_ids = pl.DeviceIdType.MESH
    grows = g_ref.shape[0]
    half = grows // 2
    rows, hidden = pre_ref.shape
    slots, columns = held.shape
    size = rows // subs

    barrier = pltpu.get_barrier_semaphore()
    for other in (mate, xn, yn):
        pl.semaphore_signal(barrier, inc=1, device_id={"text": other}, device_id_type=mesh_ids)
    for other in ((me + 1) % n, (me + n - 1) % n):
        pl.semaphore_signal(barrier, inc=1, device_id={"tile": other}, device_id_type=mesh_ids)
    loads = [pltpu.make_async_copy(pre_ref, pre, own_sem.at[0]), pltpu.make_async_copy(w_ref, weight, own_sem.at[1])]
    for copy in loads:
        copy.start()
    pl.semaphore_wait(barrier, 5)

    def part(owner, k):
        return pl.ds(pl.multiple_of(owner * grows + k * half, 16), half)

    count = [0]

    def send(src, dst, other):
        k = count[0]
        count[0] += 1
        copy = pltpu.make_async_remote_copy(
            src_ref=src, dst_ref=held.at[dst], send_sem=send_sem.at[k], recv_sem=recv_sem.at[k],
            device_id={"text": other}, device_id_type=mesh_ids)
        copy.start()
        return copy

    def mine(k):
        return g_ref.at[pl.ds(k * half, half)]

    def pass_on(owner, k, other):
        return send(held.at[part(owner, k)], part(owner, k), other)

    def use(owner, k):
        at = part(owner, k)
        term[at, :] = lax.dot_general(
            held[at, :], weight[...], (((1,), (1,)), ((), ())),
            preferred_element_type=jnp.float32).astype(term.dtype)

    def act_hop(way, step):
        block = me - step + 1 if way == 0 else me + step - 1
        k = way * (n - 1) + step - 1
        return pltpu.make_async_remote_copy(
            src_ref=act.at[block], dst_ref=act.at[block], send_sem=act_send.at[k], recv_sem=act_recv.at[k],
            device_id={"tile": me + 1 - 2 * way}, device_id_type=mesh_ids)

    def act_come(way, step):
        block = me - step if way == 0 else me + step
        k = way * (n - 1) + step - 1
        return pltpu.make_async_remote_copy(
            src_ref=act.at[block], dst_ref=act.at[block], send_sem=act_send.at[k], recv_sem=act_recv.at[k],
            device_id={"tile": me + 1 - 2 * way}, device_id_type=mesh_ids)

    def place(way):
        return me if way == 0 else n - 1 - me

    def act_forward(step):
        for way in range(2):
            i = place(way)

            @pl.when((i >= step) & (i < n - 1))
            def _():
                act_come(way, step).wait_recv()
                act_hop(way, step + 1).start()

    x0 = send(mine(0), part(t, 0), xn)
    y0 = send(mine(1), part(t, 1), yn)
    x1 = send(mine(1), part(t, 1), xn)
    y1 = send(mine(0), part(t, 0), yn)
    m0 = send(mine(0), part(t, 0), mate)
    m1 = send(mine(1), part(t, 1), mate)
    keep = [pltpu.make_async_copy(mine(k), held.at[part(t, k)], own_sem.at[2 + k]) for k in range(2)]
    for copy in keep:
        copy.start()

    loads[0].wait()
    chunk = 128

    def activate(c, carry):
        at = pl.ds(pl.multiple_of(c * chunk, chunk), chunk)
        activated, slope = gelu_parts(pre[at, :])
        grad_ref[at, :] = slope
        act[me, :, at] = activated.T.astype(jnp.bfloat16)
        return carry

    lax.fori_loop(0, rows // chunk, activate, 0)
    for way in range(2):
        @pl.when(place(way) < n - 1)
        def _():
            act_hop(way, 1).start()

    for g in range(slots // 128):
        spots[pl.ds(g * 128, 128), :] = jnp.broadcast_to(place_ref[g:g + 1, :], (128, 128)).T

    loads[1].wait()
    for k in range(2):
        keep[k].wait()
        use(t, k)
    m0.wait_recv()
    use(mate, 0)
    m1.wait_recv()
    use(mate, 1)

    x0.wait_recv()
    yf = pass_on(xn, 0, yn)
    mx0 = pass_on(xn, 0, mate)
    y0.wait_recv()
    xf = pass_on(yn, 1, xn)
    my0 = pass_on(yn, 1, mate)
    use(xn, 0)
    use(yn, 1)
    mx0.wait_recv()
    use(xn + across, 0)
    my0.wait_recv()
    use(yn + across, 1)
    act_forward(1)

    x1.wait_recv()
    mx1 = pass_on(xn, 1, mate)
    y1.wait_recv()
    my1 = pass_on(yn, 0, mate)
    use(xn, 1)
    use(yn, 0)
    mx1.wait_recv()
    use(xn + across, 1)
    my1.wait_recv()
    use(yn + across, 0)

    yf.wait_recv()
    md0 = pass_on(diag, 0, mate)
    xf.wait_recv()
    md1 = pass_on(diag, 1, mate)
    use(diag, 0)
    use(diag, 1)
    md0.wait_recv()
    use(diag + across, 0)
    md1.wait_recv()
    use(diag + across, 1)

    def hop(way, step, j):
        piece = pl.ds(pl.multiple_of(j * size, 16), size)
        k = (way * (n - 1) + step - 1) * subs + j
        return pltpu.make_async_remote_copy(
            src_ref=leave.at[way, step - 1, piece], dst_ref=arrive.at[way, step - 1, piece],
            send_sem=sum_send.at[k], recv_sem=sum_recv.at[k],
            device_id={"tile": me + 1 - 2 * way}, device_id_type=mesh_ids)

    def chosen(tile, j):
        at = pl.ds(pl.multiple_of(tile * rows + j * size, 16), size)
        column = lax.broadcasted_iota(jnp.int32, (size, slots), 1)
        pick = jnp.where(column == spots[at, :][:, :1], 1.0, 0.0).astype(jnp.bfloat16)
        return jnp.dot(pick, term[...], preferred_element_type=jnp.float32)

    def reorder(c):
        start = pl.multiple_of(c * width, width)
        column = lax.broadcasted_iota(jnp.int32, (rows, width), 1) + start
        moved = None
        for b in range(n):
            pick = jnp.where(column == spots[pl.ds(b * rows, rows), :][:, :1], 1.0, 0.0).astype(jnp.bfloat16)
            added = jnp.dot(act[b], pick, preferred_element_type=jnp.float32)
            moved = added if moved is None else moved + added
        turned[:, pl.ds(start, width)] = moved.astype(jnp.bfloat16)

    def weigh(c):
        at = pl.ds(pl.multiple_of(c * width, width), width)
        weight_ref[:, at] = jnp.dot(turned[...], held[:, at], preferred_element_type=jnp.float32)
        ones = jnp.ones((16, slots), jnp.bfloat16)
        bias_ref[:, at] = jnp.dot(ones, held[:, at], preferred_element_type=jnp.float32)[:1]

    n_own, n_turn, n_weigh = subs, slots // width, columns // width
    items = n_own + n_turn + n_weigh

    def work(c, carry):
        @pl.when(c < n_own)
        def _():
            at = pl.ds(pl.multiple_of(c * size, 16), size)
            own[at, :] = chosen(me, c)

        @pl.when(c == n_own)
        def _():
            for way in range(2):
                for step in range(1, n):
                    @pl.when((place(way) >= step) & ((place(way) == n - 1) | (step == n - 1)))
                    def _():
                        act_come(way, step).wait_recv()

        @pl.when((c >= n_own) & (c < n_own + n_turn))
        def _():
            reorder(c - n_own)

        @pl.when(c >= n_own + n_turn)
        def _():
            weigh(c - n_own - n_turn)
        return carry

    inside = (me > 0) & (me < n - 1)
    total_steps = (n - 1) * subs

    def sum_step(step, j):
        for way in range(2):
            dest = n - step if way == 0 else step - 1
            i = place(way)

            @pl.when(i < n - step)
            def _():
                piece = pl.ds(pl.multiple_of(j * size, 16), size)
                value = chosen(dest, j)
                leave[way, step - 1, piece, :] = value.astype(jnp.bfloat16)

                @pl.when(i >= 1)
                def _():
                    hop(way, step, j).wait_recv()
                    both = (leave[way, step - 1, piece, :].astype(jnp.float32)
                            + arrive[way, step - 1, piece, :].astype(jnp.float32))
                    leave[way, step - 1, piece, :] = both.astype(jnp.bfloat16)

                hop(way, step, j).start()

    for step in range(2, n - 1):
        act_forward(step)
    for step in range(1, n):
        def run(j, carry):
            sum_step(step, j)
            g = (step - 1) * subs + j
            first = jnp.where(inside, items * g // total_steps, 0)
            upto = jnp.where(inside, items * (g + 1) // total_steps, 0)
            lax.fori_loop(first, upto, work, 0)
            return carry

        lax.fori_loop(0, subs, run, 0)

    lax.fori_loop(jnp.where(inside, items, 0), items, work, 0)

    from_left = jnp.minimum(n - me, n - 1)
    from_right = jnp.minimum(me + 1, n - 1)

    def last(j, carry):
        @pl.when(me > 0)
        def _():
            hop(0, from_left, j).wait_recv()

        @pl.when(me < n - 1)
        def _():
            hop(1, from_right, j).wait_recv()

        small = 32

        def finish(c, inner):
            at = pl.ds(pl.multiple_of(j * size + c * small, 16), small)
            left = arrive[0, from_left - 1, at, :].astype(jnp.float32)
            right = arrive[1, from_right - 1, at, :].astype(jnp.float32)
            total = own[at, :] + jnp.where(me > 0, left, 0.0) + jnp.where(me < n - 1, right, 0.0)
            grad_ref[at, :] = total * grad_ref[at, :]
            return inner

        lax.fori_loop(0, size // small, finish, 0)
        return carry

    lax.fori_loop(0, subs, last, 0)

    for copy in (x0, y0, x1, y1, m0, m1, yf, mx0, xf, my0, mx1, my1, md0, md1):
        copy.wait_send()
    for way in range(2):
        for step in range(1, n):
            @pl.when((place(way) >= step - 1) & (place(way) < n - 1))
            def _():
                act_hop(way, step).wait_send()

            @pl.when(place(way) < n - step)
            def _():
                for j in range(subs):
                    hop(way, step, j).wait_send()


def fused(n, grad_seq, places, pre_act, w_out):
    rows, hidden = pre_act.shape
    slots = rows * n
    columns = grad_seq.shape[1]
    subs, width = 4, 256
    anywhere, vmem = pl.BlockSpec(memory_space=pl.ANY), pl.BlockSpec(memory_space=pltpu.VMEM)

    def kernel(*refs):
        fused_kernel(n, subs, width, *refs)

    sums = 2 * (n - 1) * subs
    return pl.pallas_call(
        kernel,
        out_shape=(jax.ShapeDtypeStruct((rows, hidden), jnp.float32),
                   jax.ShapeDtypeStruct((hidden, columns), jnp.float32),
                   jax.ShapeDtypeStruct((1, columns), jnp.float32)),
        in_specs=[anywhere, anywhere, anywhere, vmem],
        out_specs=(vmem, vmem, vmem),
        scratch_shapes=[
            pltpu.VMEM((slots, columns), jnp.bfloat16),
            pltpu.VMEM((hidden, columns), jnp.bfloat16),
            pltpu.VMEM((slots, hidden), jnp.bfloat16),
            pltpu.VMEM((rows, hidden), jnp.bfloat16),
            pltpu.VMEM((n, hidden, rows), jnp.bfloat16),
            pltpu.VMEM((hidden, slots), jnp.bfloat16),
            pltpu.VMEM((rows, hidden), jnp.float32),
            pltpu.VMEM((slots, 128), jnp.int32),
            pltpu.VMEM((2, n - 1, rows, hidden), jnp.bfloat16),
            pltpu.VMEM((2, n - 1, rows, hidden), jnp.bfloat16),
            pltpu.SemaphoreType.DMA((14,)),
            pltpu.SemaphoreType.DMA((14,)),
            pltpu.SemaphoreType.DMA((2 * (n - 1),)),
            pltpu.SemaphoreType.DMA((2 * (n - 1),)),
            pltpu.SemaphoreType.DMA((sums,)),
            pltpu.SemaphoreType.DMA((sums,)),
            pltpu.SemaphoreType.DMA((4,)),
        ],
        compiler_params=pltpu.CompilerParams(
            collective_id=0, has_side_effects=True, vmem_limit_bytes=52 * 2**20),
    )(grad_seq, w_out, pre_act, places)


def line_sum(term, me, n, rows):
    def mine(block):
        start = jnp.clip(block, 0, n - 1) * rows
        return lax.dynamic_slice_in_dim(term, start, rows, 0).astype(jnp.float32)

    total = mine(me)
    right = left = None
    for step in range(1, n):
        ahead = n - step
        out_right, out_left = mine(me + ahead), mine(me - ahead)
        if right is not None:
            out_right = out_right + right.astype(jnp.float32)
            out_left = out_left + left.astype(jnp.float32)
        hops = range(min(step, n - 1))
        right = lax.ppermute(out_right.astype(jnp.bfloat16), "tile", [(i, i + 1) for i in hops])
        left = lax.ppermute(out_left.astype(jnp.bfloat16), "tile", [(n - 1 - i, n - 2 - i) for i in hops])
    return total + right.astype(jnp.float32) + left.astype(jnp.float32)


def solution(mesh):
    n_tile, n_text = mesh.shape["tile"], mesh.shape["text"]

    def body(grad_seq, positions, pre_act, w_out):
        local_rows, hidden = pre_act.shape
        slots = positions.shape[0]
        me = lax.axis_index("tile")
        if n_text == 8:
            grad_pre, weight_term, bias = fused(n_tile, grad_seq, positions.reshape(-1, 128), pre_act, w_out)
            return (grad_pre, weight_term, bias.reshape(-1))
        gathered = lax.all_gather(grad_seq, "text", axis=0, tiled=True)
        term = jnp.einsum(
            "so,ho->sh", gathered, w_out, preferred_element_type=jnp.float32).astype(jnp.bfloat16)

        blocks = [pre_act]
        for shift in range(1, n_tile):
            ring = [(i, (i + shift) % n_tile) for i in range(n_tile)]
            blocks.append(lax.ppermute(pre_act, "tile", ring))
        blocks = lax.optimization_barrier((blocks, term))[0]
        slot = jnp.arange(slots, dtype=jnp.int32)
        turned = (me - slot // local_rows) % n_tile * local_rows + slot % local_rows
        source = jnp.zeros((slots,), jnp.int32).at[positions].set(
            turned, mode="promise_in_bounds", unique_indices=True)
        act = jnp.concatenate([gelu_parts(b)[0].astype(jnp.bfloat16) for b in blocks], axis=0)
        act_seq = rows_of(act, source)
        slope = gelu_parts(pre_act)[1]

        cut = hidden // 2 // 128 * 128
        spans = [(0, cut), (cut, hidden)] if cut else [(0, hidden)]
        summed = []
        for lo, hi in spans:
            summed.append(line_sum(rows_of(term[:, lo:hi], positions), me, n_tile, local_rows))
        weight_term = jnp.einsum("sh,so->ho", act_seq, gathered, preferred_element_type=jnp.float32)
        local_sum = jnp.sum(gathered, axis=0, dtype=jnp.float32)
        grad_pre = jnp.concatenate(summed, axis=1) * slope
        return (grad_pre, weight_term, local_sum)

    in_specs = (P("text", "tile"), P(), P("tile", "text"), P("text", "tile"))
    out_specs = (P("tile", "text"), P("text", "tile"), P("tile"))
    return jax.shard_map(body, mesh=mesh, in_specs=in_specs, out_specs=out_specs, check_vma=False)
```

```python
import jax
import jax.numpy as jnp
from jax import lax
from jax.experimental import pallas as pl
from jax.experimental.pallas import tpu as pltpu
from jax.sharding import PartitionSpec as P


def gelu_parts(pre):
    value = pre.astype(jnp.float32)
    cdf = 0.5 * (1.0 + jax.scipy.special.erf(value * 0.7071067811865476))
    activated = value * cdf
    slope = cdf + value * jnp.exp(-0.5 * value * value) * 0.3989422804014327
    return (activated, slope)


def rows_of(table, index):
    return table.at[index].get(mode="promise_in_bounds", unique_indices=True)


def fused_kernel(n, cuts, width, g_ref, w_ref, pre_ref, place_ref, grad_ref, weight_ref, bias_ref,
                 held, weight, term, pre, act, turned, own, spots, packs, ranks, arrive, leave,
                 send_sem, recv_sem, act_send, act_recv, sum_send, sum_recv, own_sem):
    t, me = lax.axis_index("text"), lax.axis_index("tile")
    core, x, y = t % 2, t // 2 % 2, t // 4
    across, beside, above = 1 - 2 * core, 2 - 4 * x, 4 - 8 * y
    mate, xn, yn = t + across, t + beside, t + above
    diag = t + beside + above
    mesh_ids = pl.DeviceIdType.MESH
    grows = g_ref.shape[0]
    half = grows // 2
    rows, hidden = pre_ref.shape
    slots, columns = held.shape
    lanes = 128
    groups = rows // lanes
    phases = len(cuts) - 1

    loads = [pltpu.make_async_copy(pre_ref, pre, own_sem.at[0]), pltpu.make_async_copy(w_ref, weight, own_sem.at[1])]
    for copy in loads:
        copy.start()
    barrier = pltpu.get_barrier_semaphore()
    for other in (mate, xn, yn):
        pl.semaphore_signal(barrier, inc=1, device_id={"text": other}, device_id_type=mesh_ids)
    for other in ((me + 1) % n, (me + n - 1) % n):
        pl.semaphore_signal(barrier, inc=1, device_id={"tile": other}, device_id_type=mesh_ids)
    pl.semaphore_wait(barrier, 5)

    def part(owner, k):
        return pl.ds(pl.multiple_of(owner * grows + k * half, 16), half)

    count = [0]

    def send(src, dst, other):
        k = count[0]
        count[0] += 1
        copy = pltpu.make_async_remote_copy(
            src_ref=src, dst_ref=held.at[dst], send_sem=send_sem.at[k], recv_sem=recv_sem.at[k],
            device_id={"text": other}, device_id_type=mesh_ids)
        copy.start()
        return copy

    def mine(k):
        return g_ref.at[pl.ds(k * half, half)]

    def pass_on(owner, k, other):
        return send(held.at[part(owner, k)], part(owner, k), other)

    def use(owner, k):
        at = part(owner, k)
        term[at, :] = lax.dot_general(
            held[at, :], weight[...], (((1,), (1,)), ((), ())),
            preferred_element_type=jnp.float32).astype(term.dtype)

    def place(way):
        return me if way == 0 else n - 1 - me

    def act_copy(way, step, block):
        k = way * (n - 1) + step - 1
        return pltpu.make_async_remote_copy(
            src_ref=act.at[block], dst_ref=act.at[block], send_sem=act_send.at[k], recv_sem=act_recv.at[k],
            device_id={"tile": me + 1 - 2 * way}, device_id_type=mesh_ids)

    def act_hop(way, step):
        return act_copy(way, step, me - step + 1 if way == 0 else me + step - 1)

    def act_come(way, step):
        return act_copy(way, step, me - step if way == 0 else me + step)

    def act_next(step):
        for way in range(2):
            i = place(way)

            @pl.when(i >= step)
            def _():
                act_come(way, step).wait_recv()

                @pl.when(i < n - 1)
                def _():
                    act_hop(way, step + 1).start()

    def reorder(block, first):
        def run(c, carry):
            start = pl.multiple_of(c * width, width)
            column = lax.broadcasted_iota(jnp.int32, (rows, width), 1) + start
            at = pl.ds(pl.multiple_of(block * rows, lanes), rows)
            pick = jnp.where(column == spots[at, :][:, :1], 1.0, 0.0).astype(jnp.bfloat16)
            moved = jnp.dot(act[block], pick, preferred_element_type=jnp.float32)
            to = (pl.ds(0, hidden), pl.ds(start, width))
            if not first:
                moved = moved + turned[to].astype(jnp.float32)
            turned[to] = moved.astype(jnp.bfloat16)
            return carry

        lax.fori_loop(0, slots // width, run, 0)

    def reorder_come(step):
        def run(way, carry):
            i = me + way * (n - 1 - 2 * me)

            @pl.when(i >= step)
            def _():
                reorder(me - step + 2 * step * way, False)
            return carry

        lax.fori_loop(0, 2, run, 0)

    x0 = send(mine(0), part(t, 0), xn)
    y0 = send(mine(1), part(t, 1), yn)
    x1 = send(mine(1), part(t, 1), xn)
    y1 = send(mine(0), part(t, 0), yn)
    m0 = send(mine(0), part(t, 0), mate)
    m1 = send(mine(1), part(t, 1), mate)
    keep = [pltpu.make_async_copy(mine(k), held.at[part(t, k)], own_sem.at[2 + k]) for k in range(2)]
    for copy in keep:
        copy.start()

    loads[0].wait()

    def activate(c, carry):
        at = pl.ds(pl.multiple_of(c * lanes, lanes), lanes)
        activated, slope = gelu_parts(pre[at, :])
        grad_ref[at, :] = slope
        act[me, :, at] = activated.T.astype(jnp.bfloat16)
        return carry

    lax.fori_loop(0, groups, activate, 0)
    for way in range(2):
        @pl.when(place(way) < n - 1)
        def _():
            act_hop(way, 1).start()

    def clear(c, carry):
        term[pl.ds(pl.multiple_of(c * half, 16), half), :] = jnp.zeros((half, hidden), jnp.bfloat16)
        return carry

    lax.fori_loop(0, slots // half, clear, 0)
    turned[pl.ds(hidden, 16), :] = jnp.ones((16, slots), jnp.bfloat16)

    loads[1].wait()
    for k in range(2):
        keep[k].wait()
        use(t, k)

    def column_of(row):
        return jnp.broadcast_to(row, (lanes, lanes)).T

    earlier = jnp.where(
        lax.broadcasted_iota(jnp.int32, (rows, rows), 0) < lax.broadcasted_iota(jnp.int32, (rows, rows), 1),
        1.0, 0.0).astype(jnp.bfloat16)

    def rank_tile(d, carry):
        pieces = [place_ref[pl.ds(d * groups + g, 1), :] for g in range(groups)]
        row = jnp.concatenate(pieces, axis=1)

        def among(start, size):
            return jnp.where((row >= start) & (row < start + size), 1.0, 0.0)

        soon = among((t - core) * grows, 2 * grows)
        for owner, k in ((xn, 0), (yn, 1)):
            soon = soon + among(owner * grows + k * half, half) + among((owner + across) * grows + k * half, half)
        later = (among((xn - core) * grows, 2 * grows) + among((yn - core) * grows, 2 * grows)
                 + among((t - core) * grows, 2 * grows) - soon)
        late = 1.0 - soon - later
        kinds = jnp.concatenate([soon, later, late, jnp.zeros((13, rows), jnp.float32)], axis=0)
        before = jnp.dot(kinds.astype(jnp.bfloat16), earlier, preferred_element_type=jnp.float32)
        n_soon = jnp.sum(soon, axis=1, keepdims=True)
        n_later = jnp.sum(later, axis=1, keepdims=True)
        rank = (soon * before[0:1] + later * (before[1:2] + n_soon)
                + late * (before[2:3] + n_soon + n_later)).astype(jnp.int32)
        high = row >> 6
        parts = jnp.concatenate([high, row - (high << 6), jnp.zeros((14, rows), jnp.int32)], axis=0)
        parts = parts.astype(jnp.float32).astype(jnp.bfloat16)
        spread = lax.broadcasted_iota(jnp.int32, (lanes, rows), 1)
        total = jnp.zeros((16, rows), jnp.float32)
        for g in range(groups):
            span = slice(g * lanes, (g + 1) * lanes)
            column = column_of(rank[:, span])

            @pl.when(d == me)
            def _():
                ranks[span, :] = column
            pick = jnp.where(spread == column[:, :1], 1.0, 0.0).astype(jnp.bfloat16)
            total = total + jnp.dot(parts[:, span], pick, preferred_element_type=jnp.float32)
        packed = (total[0:1] * 64.0 + total[1:2]).astype(jnp.int32)
        for g in range(groups):
            span = slice(g * lanes, (g + 1) * lanes)
            at = pl.ds(pl.multiple_of(d * rows + g * lanes, lanes), lanes)
            packs[at, :] = column_of(packed[:, span])
            spots[at, :] = column_of(pieces[g])
        return carry

    lax.fori_loop(0, n, rank_tile, 0)

    def chosen(table, start, size):
        at = pl.ds(pl.multiple_of(start, 16), size)
        column = lax.broadcasted_iota(jnp.int32, (size, slots), 1)
        pick = jnp.where(column == table[at, :][:, :1], 1.0, 0.0).astype(jnp.bfloat16)
        return jnp.dot(pick, term[...], preferred_element_type=jnp.float32)

    def hop(way, step, phase, slot):
        piece = pl.ds(cuts[phase], cuts[phase + 1] - cuts[phase])
        k = (way * (n - 1) + step - 1) * phases + phase
        return pltpu.make_async_remote_copy(
            src_ref=leave.at[slot, piece], dst_ref=arrive.at[way, step - 1, piece],
            send_sem=sum_send.at[k], recv_sem=sum_recv.at[k],
            device_id={"tile": me + 1 - 2 * way}, device_id_type=mesh_ids)

    def sum_step(phase, i, way, step):
        size = cuts[phase + 1] - cuts[phase]
        piece = pl.ds(cuts[phase], size)
        slot = step - 1 if i < 2 else i
        dest = (1 - way) * (n - step) + way * (step - 1)
        value = chosen(packs, dest * rows + cuts[phase], size)
        if i:
            hop(way, step, phase, slot).wait_recv()
            value = value + arrive[way, step - 1, piece, :].astype(jnp.float32)
        leave[slot, piece, :] = value.astype(jnp.bfloat16)
        hop(way, step, phase, slot).start()

    is_end = (me == 0) | (me == n - 1)
    toward = jnp.where(me * 2 < n, 0, 1)

    def sums(phase, i):
        way = toward if i < 2 else 1 - toward

        def run(step, carry):
            sum_step(phase, i, way, step)
            return carry

        lax.fori_loop(1, n - i, run, 0)

    def ends(phase):
        @pl.when(is_end)
        def _():
            sums(phase, 0)

    def middle(phase, i):
        @pl.when(jnp.logical_not(is_end))
        def _():
            sums(phase, i)

    from_left = jnp.minimum(n - me, n - 1)
    from_right = jnp.minimum(me + 1, n - 1)

    def collect(phase):
        size = cuts[phase + 1] - cuts[phase]
        column = lax.broadcasted_iota(jnp.int32, (lanes, size), 1) + cuts[phase]
        for way, there, step in ((0, me > 0, from_left), (1, me < n - 1, from_right)):
            @pl.when(there)
            def _():
                hop(way, step, phase, 0).wait_recv()

                def run(c, carry):
                    at = pl.ds(pl.multiple_of(c * lanes, lanes), lanes)
                    back = jnp.where(column == ranks[at, :][:, :1], 1.0, 0.0).astype(jnp.bfloat16)
                    own[at, :] += jnp.dot(
                        back, arrive[way, step - 1, pl.ds(cuts[phase], size), :], preferred_element_type=jnp.float32)
                    return carry

                lax.fori_loop(0, groups, run, 0)

    def keep_own(c, carry):
        at = pl.ds(pl.multiple_of(c * lanes, lanes), lanes)
        own[at, :] = chosen(spots, me * rows + c * lanes, lanes)
        return carry

    def weigh(first, upto):
        def run(c, carry):
            at = pl.ds(pl.multiple_of(c * width, width), width)
            both = jnp.dot(turned[...], held[:, at], preferred_element_type=jnp.float32)
            weight_ref[:, at] = both[:hidden]
            bias_ref[:, at] = both[hidden:hidden + 1]
            return carry

        lax.fori_loop(first, upto, run, 0)

    m0.wait_recv()
    use(mate, 0)
    m1.wait_recv()
    use(mate, 1)

    x0.wait_recv()
    yf = pass_on(xn, 0, yn)
    mx0 = pass_on(xn, 0, mate)
    y0.wait_recv()
    xf = pass_on(yn, 1, xn)
    my0 = pass_on(yn, 1, mate)
    use(xn, 0)
    use(yn, 1)
    mx0.wait_recv()
    use(xn + across, 0)
    my0.wait_recv()
    use(yn + across, 1)
    ends(0)

    reorder(me, True)
    act_next(1)
    reorder_come(1)

    x1.wait_recv()
    mx1 = pass_on(xn, 1, mate)
    y1.wait_recv()
    my1 = pass_on(yn, 0, mate)
    use(xn, 1)
    use(yn, 0)
    mx1.wait_recv()
    use(xn + across, 1)
    my1.wait_recv()
    use(yn + across, 0)
    ends(1)
    middle(0, 1)
    act_next(2)
    reorder_come(2)
    middle(0, 2)

    yf.wait_recv()
    md0 = pass_on(diag, 0, mate)
    xf.wait_recv()
    md1 = pass_on(diag, 1, mate)
    use(diag, 0)
    use(diag, 1)
    md0.wait_recv()
    use(diag + across, 0)
    md1.wait_recv()
    use(diag + across, 1)
    ends(2)

    lax.fori_loop(0, groups, keep_own, 0)
    middle(1, 1)
    middle(1, 2)
    act_next(3)
    reorder_come(3)
    collect(0)
    blocks = columns // width
    weigh(0, blocks // 2)
    middle(2, 1)
    weigh(blocks // 2, blocks * 3 // 4)
    middle(2, 2)
    collect(1)
    weigh(blocks * 3 // 4, blocks)
    collect(2)

    def finish(c, carry):
        at = pl.ds(pl.multiple_of(c * lanes, lanes), lanes)
        grad_ref[at, :] = own[at, :] * grad_ref[at, :]
        return carry

    lax.fori_loop(0, groups, finish, 0)

    for copy in (x0, y0, x1, y1, m0, m1, yf, mx0, xf, my0, mx1, my1, md0, md1):
        copy.wait_send()
    for way in range(2):
        for step in range(1, n):
            @pl.when((place(way) >= step - 1) & (place(way) < n - 1))
            def _():
                act_hop(way, step).wait_send()

            @pl.when(place(way) < n - step)
            def _():
                for phase in range(phases):
                    hop(way, step, phase, 0).wait_send()


def fused(n, cuts, grad_seq, places, pre_act, w_out):
    rows, hidden = pre_act.shape
    slots = rows * n
    columns = grad_seq.shape[1]
    width = 256
    anywhere, vmem = pl.BlockSpec(memory_space=pltpu.HBM), pl.BlockSpec(memory_space=pltpu.VMEM)

    def kernel(*refs):
        fused_kernel(n, cuts, width, *refs)

    sums = 2 * (n - 1) * (len(cuts) - 1)
    return pl.pallas_call(
        kernel,
        out_shape=(jax.ShapeDtypeStruct((rows, hidden), jnp.float32),
                   jax.ShapeDtypeStruct((hidden, columns), jnp.float32),
                   jax.ShapeDtypeStruct((1, columns), jnp.float32)),
        in_specs=[anywhere, anywhere, anywhere, vmem],
        out_specs=(vmem, vmem, vmem),
        scratch_shapes=[
            pltpu.VMEM((slots, columns), jnp.bfloat16),
            pltpu.VMEM((hidden, columns), jnp.bfloat16),
            pltpu.VMEM((slots, hidden), jnp.bfloat16),
            pltpu.VMEM((rows, hidden), jnp.bfloat16),
            pltpu.VMEM((n, hidden, rows), jnp.bfloat16),
            pltpu.VMEM((hidden + 16, slots), jnp.bfloat16),
            pltpu.VMEM((rows, hidden), jnp.float32),
            pltpu.VMEM((slots, 128), jnp.int32),
            pltpu.VMEM((slots, 128), jnp.int32),
            pltpu.VMEM((rows, 128), jnp.int32),
            pltpu.VMEM((2, n - 1, rows, hidden), jnp.bfloat16),
            pltpu.VMEM((n - 1, rows, hidden), jnp.bfloat16),
            pltpu.SemaphoreType.DMA((14,)),
            pltpu.SemaphoreType.DMA((14,)),
            pltpu.SemaphoreType.DMA((2 * (n - 1),)),
            pltpu.SemaphoreType.DMA((2 * (n - 1),)),
            pltpu.SemaphoreType.DMA((sums,)),
            pltpu.SemaphoreType.DMA((sums,)),
            pltpu.SemaphoreType.DMA((4,)),
        ],
        compiler_params=pltpu.CompilerParams(
            collective_id=0, has_side_effects=True, vmem_limit_bytes=52 * 2**20),
    )(grad_seq, w_out, pre_act, places)


def arrival_order_fits(positions, n_tile, n_text, cuts):
    pieces = 2 * n_text
    size = positions.shape[0] // pieces
    piece = jnp.arange(pieces, dtype=jnp.int32)[:, None, None] * size
    tiles = positions.reshape(1, n_tile, -1)
    held = jnp.sum((tiles >= piece) & (tiles < piece + size), axis=2, dtype=jnp.int32)
    held = held.reshape(2, 2, 2, 2, n_tile).sum(axis=2)
    flip_x, flip_y = held[:, ::-1], held[::-1]
    soon = held.sum(axis=2) + flip_x[:, :, 0] + flip_y[:, :, 1]
    later = held.sum(axis=2) + flip_x.sum(axis=2) + flip_y.sum(axis=2)
    return jnp.all((soon >= cuts[1]) & (later >= cuts[2]))


def line_sum(term, me, n, rows):
    def mine(block):
        start = jnp.clip(block, 0, n - 1) * rows
        return lax.dynamic_slice_in_dim(term, start, rows, 0).astype(jnp.float32)

    total = mine(me)
    right = left = None
    for step in range(1, n):
        ahead = n - step
        out_right, out_left = mine(me + ahead), mine(me - ahead)
        if right is not None:
            out_right = out_right + right.astype(jnp.float32)
            out_left = out_left + left.astype(jnp.float32)
        hops = range(min(step, n - 1))
        right = lax.ppermute(out_right.astype(jnp.bfloat16), "tile", [(i, i + 1) for i in hops])
        left = lax.ppermute(out_left.astype(jnp.bfloat16), "tile", [(n - 1 - i, n - 2 - i) for i in hops])
    return total + right.astype(jnp.float32) + left.astype(jnp.float32)


def solution(mesh):
    n_tile, n_text = mesh.shape["tile"], mesh.shape["text"]

    def plain(grad_seq, positions, pre_act, w_out):
        local_rows, hidden = pre_act.shape
        slots = positions.shape[0]
        me = lax.axis_index("tile")
        gathered = lax.all_gather(grad_seq, "text", axis=0, tiled=True)
        term = jnp.einsum(
            "so,ho->sh", gathered, w_out, preferred_element_type=jnp.float32).astype(jnp.bfloat16)

        blocks = [pre_act]
        for shift in range(1, n_tile):
            ring = [(i, (i + shift) % n_tile) for i in range(n_tile)]
            blocks.append(lax.ppermute(pre_act, "tile", ring))
        blocks = lax.optimization_barrier((blocks, term))[0]
        slot = jnp.arange(slots, dtype=jnp.int32)
        turned = (me - slot // local_rows) % n_tile * local_rows + slot % local_rows
        source = jnp.zeros((slots,), jnp.int32).at[positions].set(
            turned, mode="promise_in_bounds", unique_indices=True)
        act = jnp.concatenate([gelu_parts(b)[0].astype(jnp.bfloat16) for b in blocks], axis=0)
        act_seq = rows_of(act, source)
        slope = gelu_parts(pre_act)[1]

        cut = hidden // 2 // 128 * 128
        spans = [(0, cut), (cut, hidden)] if cut else [(0, hidden)]
        summed = []
        for lo, hi in spans:
            summed.append(line_sum(rows_of(term[:, lo:hi], positions), me, n_tile, local_rows))
        weight_term = jnp.einsum("sh,so->ho", act_seq, gathered, preferred_element_type=jnp.float32)
        local_sum = jnp.sum(gathered, axis=0, dtype=jnp.float32)
        grad_pre = jnp.concatenate(summed, axis=1) * slope
        return (grad_pre, weight_term, local_sum)

    def body(grad_seq, positions, pre_act, w_out):
        if n_tile != 4 or n_text != 8:
            return plain(grad_seq, positions, pre_act, w_out)
        rows = pre_act.shape[0]
        cuts = (0, rows * 2 // 5 // 16 * 16, rows * 13 // 20 // 16 * 16, rows)

        def quick(grad_seq, positions, pre_act, w_out):
            grad_pre, weight_term, bias = fused(n_tile, cuts, grad_seq, positions.reshape(-1, 128), pre_act, w_out)
            return (grad_pre, weight_term, bias.reshape(-1))

        fits = arrival_order_fits(positions, n_tile, n_text, cuts)
        return lax.cond(fits, quick, plain, grad_seq, positions, pre_act, w_out)

    in_specs = (P("text", "tile"), P(), P("tile", "text"), P("text", "tile"))
    out_specs = (P("tile", "text"), P("text", "tile"), P("tile"))
    return jax.shard_map(body, mesh=mesh, in_specs=in_specs, out_specs=out_specs, check_vma=False)
```

```python
import jax
import jax.numpy as jnp
from jax import lax
from jax.experimental import pallas as pl
from jax.experimental.pallas import tpu as pltpu
from jax.sharding import PartitionSpec as P


def gelu_parts(pre):
    value = pre.astype(jnp.float32)
    cdf = 0.5 * (1.0 + jax.scipy.special.erf(value * 0.7071067811865476))
    activated = value * cdf
    slope = cdf + value * jnp.exp(-0.5 * value * value) * 0.3989422804014327
    return (activated, slope)


def rows_of(table, index):
    return table.at[index].get(mode="promise_in_bounds", unique_indices=True)


def fused_kernel(n, cuts, width, g_ref, w_ref, pre_ref, place_ref, grad_ref, weight_ref, bias_ref,
                 held, weight, term, pre, act, turned, own, spots, packs, ranks, arrive, leave,
                 send_sem, recv_sem, act_send, act_recv, sum_send, sum_recv, own_sem):
    t, me = lax.axis_index("text"), lax.axis_index("tile")
    core, x, y = t % 2, t // 2 % 2, t // 4
    across, beside, above = 1 - 2 * core, 2 - 4 * x, 4 - 8 * y
    mate, xn, yn = t + across, t + beside, t + above
    diag = t + beside + above
    mesh_ids = pl.DeviceIdType.MESH
    grows = g_ref.shape[0]
    half = grows // 2
    rows, hidden = pre_ref.shape
    slots, columns = held.shape
    lanes = 128
    groups = rows // lanes
    phases = len(cuts) - 1

    loads = [pltpu.make_async_copy(pre_ref, pre, own_sem.at[0]), pltpu.make_async_copy(w_ref, weight, own_sem.at[1])]
    for copy in loads:
        copy.start()
    barrier = pltpu.get_barrier_semaphore()
    for other in (mate, xn, yn):
        pl.semaphore_signal(barrier, inc=1, device_id={"text": other}, device_id_type=mesh_ids)
    for other in ((me + 1) % n, (me + n - 1) % n):
        pl.semaphore_signal(barrier, inc=1, device_id={"tile": other}, device_id_type=mesh_ids)
    pl.semaphore_wait(barrier, 5)

    def part(owner, k):
        return pl.ds(pl.multiple_of(owner * grows + k * half, 16), half)

    count = [0]

    def send(src, dst, other):
        k = count[0]
        count[0] += 1
        copy = pltpu.make_async_remote_copy(
            src_ref=src, dst_ref=held.at[dst], send_sem=send_sem.at[k], recv_sem=recv_sem.at[k],
            device_id={"text": other}, device_id_type=mesh_ids)
        copy.start()
        return copy

    def mine(k):
        return g_ref.at[pl.ds(k * half, half)]

    def pass_on(owner, k, other):
        return send(held.at[part(owner, k)], part(owner, k), other)

    def use(owner, k):
        at = part(owner, k)
        term[at, :] = lax.dot_general(
            held[at, :], weight[...], (((1,), (1,)), ((), ())),
            preferred_element_type=jnp.float32).astype(term.dtype)

    def place(way):
        return me if way == 0 else n - 1 - me

    def act_copy(way, step, block):
        k = way * (n - 1) + step - 1
        return pltpu.make_async_remote_copy(
            src_ref=act.at[block], dst_ref=act.at[block], send_sem=act_send.at[k], recv_sem=act_recv.at[k],
            device_id={"tile": me + 1 - 2 * way}, device_id_type=mesh_ids)

    def act_hop(way, step):
        return act_copy(way, step, me - step + 1 if way == 0 else me + step - 1)

    def act_come(way, step):
        return act_copy(way, step, me - step if way == 0 else me + step)

    def act_next(step):
        for way in range(2):
            i = place(way)

            @pl.when(i >= step)
            def _():
                act_come(way, step).wait_recv()

                @pl.when(i < n - 1)
                def _():
                    act_hop(way, step + 1).start()

    def reorder(block, first):
        def run(c, carry):
            start = pl.multiple_of(c * width, width)
            column = lax.broadcasted_iota(jnp.int32, (rows, width), 1) + start
            at = pl.ds(pl.multiple_of(block * rows, lanes), rows)
            pick = jnp.where(column == spots[at, :][:, :1], 1.0, 0.0).astype(jnp.bfloat16)
            moved = jnp.dot(act[block], pick, preferred_element_type=jnp.float32)
            to = (pl.ds(0, hidden), pl.ds(start, width))
            if not first:
                moved = moved + turned[to].astype(jnp.float32)
            turned[to] = moved.astype(jnp.bfloat16)
            return carry

        lax.fori_loop(0, slots // width, run, 0)

    def reorder_come(step):
        def run(way, carry):
            i = me + way * (n - 1 - 2 * me)

            @pl.when(i >= step)
            def _():
                reorder(me - step + 2 * step * way, False)
            return carry

        lax.fori_loop(0, 2, run, 0)

    x0 = send(mine(0), part(t, 0), xn)
    y0 = send(mine(1), part(t, 1), yn)
    x1 = send(mine(1), part(t, 1), xn)
    y1 = send(mine(0), part(t, 0), yn)
    m0 = send(mine(0), part(t, 0), mate)
    m1 = send(mine(1), part(t, 1), mate)
    keep = [pltpu.make_async_copy(mine(k), held.at[part(t, k)], own_sem.at[2 + k]) for k in range(2)]
    for copy in keep:
        copy.start()

    loads[0].wait()

    def activate(c, carry):
        at = pl.ds(pl.multiple_of(c * lanes, lanes), lanes)
        activated, slope = gelu_parts(pre[at, :])
        grad_ref[at, :] = slope
        act[me, :, at] = activated.T.astype(jnp.bfloat16)
        return carry

    lax.fori_loop(0, groups, activate, 0)
    for way in range(2):
        @pl.when(place(way) < n - 1)
        def _():
            act_hop(way, 1).start()

    def clear(c, carry):
        term[pl.ds(pl.multiple_of(c * half, 16), half), :] = jnp.zeros((half, hidden), jnp.bfloat16)
        return carry

    lax.fori_loop(0, slots // half, clear, 0)
    turned[pl.ds(hidden, 16), :] = jnp.ones((16, slots), jnp.bfloat16)

    loads[1].wait()
    for k in range(2):
        keep[k].wait()
        use(t, k)

    def column_of(row):
        return jnp.broadcast_to(row, (lanes, lanes)).T

    earlier = jnp.where(
        lax.broadcasted_iota(jnp.int32, (rows, rows), 0) < lax.broadcasted_iota(jnp.int32, (rows, rows), 1),
        1.0, 0.0).astype(jnp.bfloat16)

    def rank_tile(d, carry):
        pieces = [place_ref[pl.ds(d * groups + g, 1), :] for g in range(groups)]
        row = jnp.concatenate(pieces, axis=1)

        def among(start, size):
            return jnp.where((row >= start) & (row < start + size), 1.0, 0.0)

        soon = among((t - core) * grows, 2 * grows)
        for owner, k in ((xn, 0), (yn, 1)):
            soon = soon + among(owner * grows + k * half, half) + among((owner + across) * grows + k * half, half)
        later = (among((xn - core) * grows, 2 * grows) + among((yn - core) * grows, 2 * grows)
                 + among((t - core) * grows, 2 * grows) - soon)
        late = 1.0 - soon - later
        kinds = jnp.concatenate([soon, later, late, jnp.zeros((13, rows), jnp.float32)], axis=0)
        before = jnp.dot(kinds.astype(jnp.bfloat16), earlier, preferred_element_type=jnp.float32)
        n_soon = jnp.sum(soon, axis=1, keepdims=True)
        n_later = jnp.sum(later, axis=1, keepdims=True)
        rank = (soon * before[0:1] + later * (before[1:2] + n_soon)
                + late * (before[2:3] + n_soon + n_later)).astype(jnp.int32)
        high = row >> 6
        parts = jnp.concatenate([high, row - (high << 6), jnp.zeros((14, rows), jnp.int32)], axis=0)
        parts = parts.astype(jnp.float32).astype(jnp.bfloat16)
        spread = lax.broadcasted_iota(jnp.int32, (lanes, rows), 1)
        total = jnp.zeros((16, rows), jnp.float32)
        for g in range(groups):
            span = slice(g * lanes, (g + 1) * lanes)
            column = column_of(rank[:, span])

            @pl.when(d == me)
            def _():
                ranks[span, :] = column
            pick = jnp.where(spread == column[:, :1], 1.0, 0.0).astype(jnp.bfloat16)
            total = total + jnp.dot(parts[:, span], pick, preferred_element_type=jnp.float32)
        packed = (total[0:1] * 64.0 + total[1:2]).astype(jnp.int32)
        for g in range(groups):
            span = slice(g * lanes, (g + 1) * lanes)
            at = pl.ds(pl.multiple_of(d * rows + g * lanes, lanes), lanes)
            packs[at, :] = column_of(packed[:, span])
            spots[at, :] = column_of(pieces[g])
        return carry

    lax.fori_loop(0, n, rank_tile, 0)

    def chosen(table, start, size):
        at = pl.ds(pl.multiple_of(start, 16), size)
        column = lax.broadcasted_iota(jnp.int32, (size, slots), 1)
        pick = jnp.where(column == table[at, :][:, :1], 1.0, 0.0).astype(jnp.bfloat16)
        return jnp.dot(pick, term[...], preferred_element_type=jnp.float32)

    def hop(way, step, phase, slot):
        piece = pl.ds(cuts[phase], cuts[phase + 1] - cuts[phase])
        k = (way * (n - 1) + step - 1) * phases + phase
        return pltpu.make_async_remote_copy(
            src_ref=leave.at[slot, piece], dst_ref=arrive.at[way, step - 1, piece],
            send_sem=sum_send.at[k], recv_sem=sum_recv.at[k],
            device_id={"tile": me + 1 - 2 * way}, device_id_type=mesh_ids)

    def sum_step(phase, i, way, step):
        size = cuts[phase + 1] - cuts[phase]
        piece = pl.ds(cuts[phase], size)
        slot = step - 1 if i < 2 else i
        dest = (1 - way) * (n - step) + way * (step - 1)
        value = chosen(packs, dest * rows + cuts[phase], size)
        if i:
            hop(way, step, phase, slot).wait_recv()
            value = value + arrive[way, step - 1, piece, :].astype(jnp.float32)
        leave[slot, piece, :] = value.astype(jnp.bfloat16)
        hop(way, step, phase, slot).start()

    is_end = (me == 0) | (me == n - 1)
    toward = jnp.where(me * 2 < n, 0, 1)

    def sums(phase, i):
        way = toward if i < 2 else 1 - toward

        def run(step, carry):
            sum_step(phase, i, way, step)
            return carry

        lax.fori_loop(1, n - i, run, 0)

    def ends(phase):
        @pl.when(is_end)
        def _():
            sums(phase, 0)

    def middle(phase, i):
        @pl.when(jnp.logical_not(is_end))
        def _():
            sums(phase, i)

    from_left = jnp.minimum(n - me, n - 1)
    from_right = jnp.minimum(me + 1, n - 1)

    def collect(phase):
        size = cuts[phase + 1] - cuts[phase]
        column = lax.broadcasted_iota(jnp.int32, (lanes, size), 1) + cuts[phase]
        for way, there, step in ((0, me > 0, from_left), (1, me < n - 1, from_right)):
            @pl.when(there)
            def _():
                hop(way, step, phase, 0).wait_recv()

                def run(c, carry):
                    at = pl.ds(pl.multiple_of(c * lanes, lanes), lanes)
                    back = jnp.where(column == ranks[at, :][:, :1], 1.0, 0.0).astype(jnp.bfloat16)
                    own[at, :] += jnp.dot(
                        back, arrive[way, step - 1, pl.ds(cuts[phase], size), :], preferred_element_type=jnp.float32)
                    return carry

                lax.fori_loop(0, groups, run, 0)

    def keep_own(c, carry):
        at = pl.ds(pl.multiple_of(c * lanes, lanes), lanes)
        own[at, :] = chosen(spots, me * rows + c * lanes, lanes)
        return carry

    def weigh(first, upto):
        def run(c, carry):
            at = pl.ds(pl.multiple_of(c * width, width), width)
            both = jnp.dot(turned[...], held[:, at], preferred_element_type=jnp.float32)
            weight_ref[:, at] = both[:hidden]
            bias_ref[:, at] = both[hidden:hidden + 1]
            return carry

        lax.fori_loop(first, upto, run, 0)

    m0.wait_recv()
    use(mate, 0)
    m1.wait_recv()
    use(mate, 1)

    x0.wait_recv()
    yf = pass_on(xn, 0, yn)
    mx0 = pass_on(xn, 0, mate)
    y0.wait_recv()
    xf = pass_on(yn, 1, xn)
    my0 = pass_on(yn, 1, mate)
    use(xn, 0)
    use(yn, 1)
    mx0.wait_recv()
    use(xn + across, 0)
    my0.wait_recv()
    use(yn + across, 1)
    ends(0)

    reorder(me, True)
    act_next(1)
    reorder_come(1)

    x1.wait_recv()
    mx1 = pass_on(xn, 1, mate)
    y1.wait_recv()
    my1 = pass_on(yn, 0, mate)
    use(xn, 1)
    use(yn, 0)
    mx1.wait_recv()
    use(xn + across, 1)
    my1.wait_recv()
    use(yn + across, 0)
    ends(1)
    middle(0, 1)
    act_next(2)
    reorder_come(2)
    middle(0, 2)

    yf.wait_recv()
    md0 = pass_on(diag, 0, mate)
    xf.wait_recv()
    md1 = pass_on(diag, 1, mate)
    use(diag, 0)
    use(diag, 1)
    md0.wait_recv()
    use(diag + across, 0)
    md1.wait_recv()
    use(diag + across, 1)
    ends(2)

    lax.fori_loop(0, groups, keep_own, 0)
    middle(1, 1)
    middle(1, 2)
    act_next(3)
    reorder_come(3)
    collect(0)
    blocks = columns // width
    weigh(0, blocks // 2)
    middle(2, 1)
    weigh(blocks // 2, blocks * 3 // 4)
    middle(2, 2)
    collect(1)
    weigh(blocks * 3 // 4, blocks)
    collect(2)

    def finish(c, carry):
        at = pl.ds(pl.multiple_of(c * lanes, lanes), lanes)
        grad_ref[at, :] = own[at, :] * grad_ref[at, :]
        return carry

    lax.fori_loop(0, groups, finish, 0)

    for copy in (x0, y0, x1, y1, m0, m1, yf, mx0, xf, my0, mx1, my1, md0, md1):
        copy.wait_send()
    for way in range(2):
        for step in range(1, n):
            @pl.when((place(way) >= step - 1) & (place(way) < n - 1))
            def _():
                act_hop(way, step).wait_send()

            @pl.when(place(way) < n - step)
            def _():
                for phase in range(phases):
                    hop(way, step, phase, 0).wait_send()


def fused(n, cuts, grad_seq, places, pre_act, w_out):
    rows, hidden = pre_act.shape
    slots = rows * n
    columns = grad_seq.shape[1]
    width = 256
    anywhere, vmem = pl.BlockSpec(memory_space=pltpu.HBM), pl.BlockSpec(memory_space=pltpu.VMEM)

    def kernel(*refs):
        fused_kernel(n, cuts, width, *refs)

    sums = 2 * (n - 1) * (len(cuts) - 1)
    return pl.pallas_call(
        kernel,
        out_shape=(jax.ShapeDtypeStruct((rows, hidden), jnp.float32),
                   jax.ShapeDtypeStruct((hidden, columns), jnp.float32),
                   jax.ShapeDtypeStruct((1, columns), jnp.float32)),
        in_specs=[anywhere, anywhere, anywhere, vmem],
        out_specs=(vmem, vmem, vmem),
        scratch_shapes=[
            pltpu.VMEM((slots, columns), jnp.bfloat16),
            pltpu.VMEM((hidden, columns), jnp.bfloat16),
            pltpu.VMEM((slots, hidden), jnp.bfloat16),
            pltpu.VMEM((rows, hidden), jnp.bfloat16),
            pltpu.VMEM((n, hidden, rows), jnp.bfloat16),
            pltpu.VMEM((hidden + 16, slots), jnp.bfloat16),
            pltpu.VMEM((rows, hidden), jnp.float32),
            pltpu.VMEM((slots, 128), jnp.int32),
            pltpu.VMEM((slots, 128), jnp.int32),
            pltpu.VMEM((rows, 128), jnp.int32),
            pltpu.VMEM((2, n - 1, rows, hidden), jnp.bfloat16),
            pltpu.VMEM((n - 1, rows, hidden), jnp.bfloat16),
            pltpu.SemaphoreType.DMA((14,)),
            pltpu.SemaphoreType.DMA((14,)),
            pltpu.SemaphoreType.DMA((2 * (n - 1),)),
            pltpu.SemaphoreType.DMA((2 * (n - 1),)),
            pltpu.SemaphoreType.DMA((sums,)),
            pltpu.SemaphoreType.DMA((sums,)),
            pltpu.SemaphoreType.DMA((4,)),
        ],
        compiler_params=pltpu.CompilerParams(
            collective_id=0, has_side_effects=True, vmem_limit_bytes=52 * 2**20),
    )(grad_seq, w_out, pre_act, places)


def arrival_order_fits(positions, n_tile, n_text, cuts):
    pieces = 2 * n_text
    size = positions.shape[0] // pieces
    piece = jnp.arange(pieces, dtype=jnp.int32)[:, None, None] * size
    tiles = positions.reshape(1, n_tile, -1)
    held = jnp.sum((tiles >= piece) & (tiles < piece + size), axis=2, dtype=jnp.int32)
    held = held.reshape(2, 2, 2, 2, n_tile).sum(axis=2)
    flip_x, flip_y = held[:, ::-1], held[::-1]
    soon = held.sum(axis=2) + flip_x[:, :, 0] + flip_y[:, :, 1]
    later = held.sum(axis=2) + flip_x.sum(axis=2) + flip_y.sum(axis=2)
    return jnp.all((soon >= cuts[1]) & (later >= cuts[2]))


def line_sum(term, me, n, rows):
    def mine(block):
        start = jnp.clip(block, 0, n - 1) * rows
        return lax.dynamic_slice_in_dim(term, start, rows, 0).astype(jnp.float32)

    total = mine(me)
    right = left = None
    for step in range(1, n):
        ahead = n - step
        out_right, out_left = mine(me + ahead), mine(me - ahead)
        if right is not None:
            out_right = out_right + right.astype(jnp.float32)
            out_left = out_left + left.astype(jnp.float32)
        hops = range(min(step, n - 1))
        right = lax.ppermute(out_right.astype(jnp.bfloat16), "tile", [(i, i + 1) for i in hops])
        left = lax.ppermute(out_left.astype(jnp.bfloat16), "tile", [(n - 1 - i, n - 2 - i) for i in hops])
    return total + right.astype(jnp.float32) + left.astype(jnp.float32)


def solution(mesh):
    n_tile, n_text = mesh.shape["tile"], mesh.shape["text"]

    def whole_sequence(grad_seq, n_text, n_tile):
        if n_tile != 4 or n_text != 8:
            return lax.all_gather(grad_seq, "text", axis=0, tiled=True)
        rows = grad_seq.shape[0]
        t = lax.axis_index("text")
        gathered = jnp.zeros((rows * n_text, grad_seq.shape[1]), grad_seq.dtype)
        for shift in range(n_text):
            ring = [(i, (i + shift) % n_text) for i in range(n_text)]
            block = lax.ppermute(grad_seq, "text", ring) if shift else grad_seq
            gathered = lax.dynamic_update_slice_in_dim(gathered, block, (t - shift) % n_text * rows, 0)
        return gathered

    def plain(grad_seq, positions, pre_act, w_out):
        local_rows, hidden = pre_act.shape
        slots = positions.shape[0]
        me = lax.axis_index("tile")
        gathered = whole_sequence(grad_seq, n_text, n_tile)
        term = jnp.einsum(
            "so,ho->sh", gathered, w_out, preferred_element_type=jnp.float32).astype(jnp.bfloat16)

        blocks = [pre_act]
        for shift in range(1, n_tile):
            ring = [(i, (i + shift) % n_tile) for i in range(n_tile)]
            blocks.append(lax.ppermute(pre_act, "tile", ring))
        blocks = lax.optimization_barrier((blocks, term))[0]
        slot = jnp.arange(slots, dtype=jnp.int32)
        turned = (me - slot // local_rows) % n_tile * local_rows + slot % local_rows
        source = jnp.zeros((slots,), jnp.int32).at[positions].set(
            turned, mode="promise_in_bounds", unique_indices=True)
        act = jnp.concatenate([gelu_parts(b)[0].astype(jnp.bfloat16) for b in blocks], axis=0)
        act_seq = rows_of(act, source)
        slope = gelu_parts(pre_act)[1]

        cut = hidden // 2 // 128 * 128
        spans = [(0, cut), (cut, hidden)] if cut else [(0, hidden)]
        summed = []
        for lo, hi in spans:
            summed.append(line_sum(rows_of(term[:, lo:hi], positions), me, n_tile, local_rows))
        weight_term = jnp.einsum("sh,so->ho", act_seq, gathered, preferred_element_type=jnp.float32)
        local_sum = jnp.sum(gathered, axis=0, dtype=jnp.float32)
        grad_pre = jnp.concatenate(summed, axis=1) * slope
        return (grad_pre, weight_term, local_sum)

    def body(grad_seq, positions, pre_act, w_out):
        if n_tile != 4 or n_text != 8:
            return plain(grad_seq, positions, pre_act, w_out)
        rows = pre_act.shape[0]
        cuts = (0, rows * 2 // 5 // 16 * 16, rows * 13 // 20 // 16 * 16, rows)

        def quick(grad_seq, positions, pre_act, w_out):
            grad_pre, weight_term, bias = fused(n_tile, cuts, grad_seq, positions.reshape(-1, 128), pre_act, w_out)
            return (grad_pre, weight_term, bias.reshape(-1))

        fits = arrival_order_fits(positions, n_tile, n_text, cuts)
        return lax.cond(fits, quick, plain, grad_seq, positions, pre_act, w_out)

    in_specs = (P("text", "tile"), P(), P("tile", "text"), P("text", "tile"))
    out_specs = (P("tile", "text"), P("text", "tile"), P("tile"))
    return jax.shard_map(body, mesh=mesh, in_specs=in_specs, out_specs=out_specs, check_vma=False)
```

```python
import jax
import jax.numpy as jnp
from jax import lax
from jax.experimental import pallas as pl
from jax.experimental.pallas import tpu as pltpu
from jax.sharding import PartitionSpec as P


def gelu_parts(pre):
    value = pre.astype(jnp.float32)
    cdf = 0.5 * (1.0 + jax.scipy.special.erf(value * 0.7071067811865476))
    activated = value * cdf
    slope = cdf + value * jnp.exp(-0.5 * value * value) * 0.3989422804014327
    return (activated, slope)


def rows_of(table, index):
    return table.at[index].get(mode="promise_in_bounds", unique_indices=True)


def fused_kernel(n, cuts, width, g_ref, w_ref, pre_ref, place_ref, grad_ref, weight_ref, bias_ref,
                 held, weight, term, pre, act, turned, own, spots, packs, ranks, arrive, leave,
                 send_sem, recv_sem, act_send, act_recv, sum_send, sum_recv, own_sem):
    t, me = lax.axis_index("text"), lax.axis_index("tile")
    core, x, y = t % 2, t // 2 % 2, t // 4
    across, beside, above = 1 - 2 * core, 2 - 4 * x, 4 - 8 * y
    mate, xn, yn = t + across, t + beside, t + above
    diag = t + beside + above
    mesh_ids = pl.DeviceIdType.MESH
    grows = g_ref.shape[0]
    half = grows // 2
    rows, hidden = pre_ref.shape
    slots, columns = held.shape
    lanes = 128
    groups = rows // lanes
    phases = len(cuts) - 1

    loads = [pltpu.make_async_copy(pre_ref, pre, own_sem.at[0]), pltpu.make_async_copy(w_ref, weight, own_sem.at[1])]
    for copy in loads:
        copy.start()
    barrier = pltpu.get_barrier_semaphore()
    for other in (mate, xn, yn):
        pl.semaphore_signal(barrier, inc=1, device_id={"text": other}, device_id_type=mesh_ids)
    for other in ((me + 1) % n, (me + n - 1) % n):
        pl.semaphore_signal(barrier, inc=1, device_id={"tile": other}, device_id_type=mesh_ids)
    pl.semaphore_wait(barrier, 5)

    def part(owner, k):
        return pl.ds(pl.multiple_of(owner * grows + k * half, 16), half)

    count = [0]

    def send(src, dst, other):
        k = count[0]
        count[0] += 1
        copy = pltpu.make_async_remote_copy(
            src_ref=src, dst_ref=held.at[dst], send_sem=send_sem.at[k], recv_sem=recv_sem.at[k],
            device_id={"text": other}, device_id_type=mesh_ids)
        copy.start()
        return copy

    def mine(k):
        return g_ref.at[pl.ds(k * half, half)]

    def pass_on(owner, k, other):
        return send(held.at[part(owner, k)], part(owner, k), other)

    def use(*parts):
        spans = [part(owner, k) for owner, k in parts]
        value = lax.dot_general(
            jnp.concatenate([held[at, :] for at in spans], axis=0), weight[...], (((1,), (1,)), ((), ())),
            preferred_element_type=jnp.float32).astype(term.dtype)
        for c, at in enumerate(spans):
            term[at, :] = value[c * half:(c + 1) * half]

    def place(way):
        return me if way == 0 else n - 1 - me

    def act_copy(way, step, block):
        k = way * (n - 1) + step - 1
        return pltpu.make_async_remote_copy(
            src_ref=act.at[block], dst_ref=act.at[block], send_sem=act_send.at[k], recv_sem=act_recv.at[k],
            device_id={"tile": me + 1 - 2 * way}, device_id_type=mesh_ids)

    def act_hop(way, step):
        return act_copy(way, step, me - step + 1 if way == 0 else me + step - 1)

    def act_come(way, step):
        return act_copy(way, step, me - step if way == 0 else me + step)

    def act_next(step):
        for way in range(2):
            i = place(way)

            @pl.when(i >= step)
            def _():
                act_come(way, step).wait_recv()

                @pl.when(i < n - 1)
                def _():
                    act_hop(way, step + 1).start()

    def reorder(block, first):
        def run(c, carry):
            start = pl.multiple_of(c * width, width)
            column = lax.broadcasted_iota(jnp.int32, (rows, width), 1) + start
            at = pl.ds(pl.multiple_of(block * rows, lanes), rows)
            pick = jnp.where(column == spots[at, :][:, :1], 1.0, 0.0).astype(jnp.bfloat16)
            moved = jnp.dot(act[block], pick, preferred_element_type=jnp.float32)
            to = (pl.ds(0, hidden), pl.ds(start, width))
            if not first:
                moved = moved + turned[to].astype(jnp.float32)
            turned[to] = moved.astype(jnp.bfloat16)
            return carry

        lax.fori_loop(0, slots // width, run, 0)

    def reorder_come(step):
        def run(way, carry):
            i = me + way * (n - 1 - 2 * me)

            @pl.when(i >= step)
            def _():
                reorder(me - step + 2 * step * way, False)
            return carry

        lax.fori_loop(0, 2, run, 0)

    x0 = send(mine(0), part(t, 0), xn)
    y0 = send(mine(1), part(t, 1), yn)
    x1 = send(mine(1), part(t, 1), xn)
    y1 = send(mine(0), part(t, 0), yn)
    m0 = send(mine(0), part(t, 0), mate)
    m1 = send(mine(1), part(t, 1), mate)
    keep = [pltpu.make_async_copy(mine(k), held.at[part(t, k)], own_sem.at[2 + k]) for k in range(2)]
    for copy in keep:
        copy.start()

    loads[0].wait()

    def activate(c, carry):
        at = pl.ds(pl.multiple_of(c * lanes, lanes), lanes)
        activated, slope = gelu_parts(pre[at, :])
        grad_ref[at, :] = slope
        act[me, :, at] = activated.T.astype(jnp.bfloat16)
        return carry

    lax.fori_loop(0, groups, activate, 0)
    for way in range(2):
        @pl.when(place(way) < n - 1)
        def _():
            act_hop(way, 1).start()

    def clear(c, carry):
        term[pl.ds(pl.multiple_of(c * half, 16), half), :] = jnp.zeros((half, hidden), jnp.bfloat16)
        return carry

    lax.fori_loop(0, slots // half, clear, 0)
    turned[pl.ds(hidden, 16), :] = jnp.ones((16, slots), jnp.bfloat16)

    loads[1].wait()
    for k in range(2):
        keep[k].wait()

    def column_of(row):
        return jnp.broadcast_to(row, (lanes, lanes)).T

    earlier = jnp.where(
        lax.broadcasted_iota(jnp.int32, (rows, rows), 0) < lax.broadcasted_iota(jnp.int32, (rows, rows), 1),
        1.0, 0.0).astype(jnp.bfloat16)

    def rank_tile(d, carry):
        pieces = [place_ref[pl.ds(d * groups + g, 1), :] for g in range(groups)]
        row = jnp.concatenate(pieces, axis=1)

        def among(start, size):
            return jnp.where((row >= start) & (row < start + size), 1.0, 0.0)

        soon = among((t - core) * grows, 2 * grows)
        for owner, k in ((xn, 0), (yn, 1)):
            soon = soon + among(owner * grows + k * half, half) + among((owner + across) * grows + k * half, half)
        later = (among((xn - core) * grows, 2 * grows) + among((yn - core) * grows, 2 * grows)
                 + among((t - core) * grows, 2 * grows) - soon)
        late = 1.0 - soon - later
        kinds = jnp.concatenate([soon, later, late, jnp.zeros((13, rows), jnp.float32)], axis=0)
        before = jnp.dot(kinds.astype(jnp.bfloat16), earlier, preferred_element_type=jnp.float32)
        n_soon = jnp.sum(soon, axis=1, keepdims=True)
        n_later = jnp.sum(later, axis=1, keepdims=True)
        rank = (soon * before[0:1] + later * (before[1:2] + n_soon)
                + late * (before[2:3] + n_soon + n_later)).astype(jnp.int32)
        high = row >> 6
        parts = jnp.concatenate([high, row - (high << 6), jnp.zeros((14, rows), jnp.int32)], axis=0)
        parts = parts.astype(jnp.float32).astype(jnp.bfloat16)
        spread = lax.broadcasted_iota(jnp.int32, (lanes, rows), 1)
        total = jnp.zeros((16, rows), jnp.float32)
        for g in range(groups):
            span = slice(g * lanes, (g + 1) * lanes)
            column = column_of(rank[:, span])

            @pl.when(d == me)
            def _():
                ranks[span, :] = column
            pick = jnp.where(spread == column[:, :1], 1.0, 0.0).astype(jnp.bfloat16)
            total = total + jnp.dot(parts[:, span], pick, preferred_element_type=jnp.float32)
        packed = (total[0:1] * 64.0 + total[1:2]).astype(jnp.int32)
        for g in range(groups):
            span = slice(g * lanes, (g + 1) * lanes)
            at = pl.ds(pl.multiple_of(d * rows + g * lanes, lanes), lanes)
            packs[at, :] = column_of(packed[:, span])
            spots[at, :] = column_of(pieces[g])
        return carry

    lax.fori_loop(0, n, rank_tile, 0)

    is_end = (me == 0) | (me == n - 1)
    toward = jnp.where(me * 2 < n, 0, 1)

    def chosen(table, starts, size):
        spans = [pl.ds(pl.multiple_of(start, 16), size) for start in starts]
        column = lax.broadcasted_iota(jnp.int32, (size, slots), 1)
        picks = [jnp.where(column == table[at, :][:, :1], 1.0, 0.0).astype(jnp.bfloat16) for at in spans]
        pick = jnp.concatenate(picks, axis=0) if len(picks) > 1 else picks[0]
        return jnp.dot(pick, term[...], preferred_element_type=jnp.float32)

    def pick_sums(phase):
        size = cuts[phase + 1] - cuts[phase]
        tiles = []
        for slot in range(n - 1):
            first = (1 - toward) * (n - 1 - slot) + toward * slot
            tiles.append(first if slot < n - 2 else jnp.where(is_end, first, toward * (n - 1)))
        value = chosen(packs, [tile * rows + cuts[phase] for tile in tiles], size).astype(jnp.bfloat16)
        for slot in range(n - 1):
            leave[slot, pl.ds(cuts[phase], size), :] = value[slot * size:(slot + 1) * size]

    def hop(way, step, phase, slot):
        piece = pl.ds(cuts[phase], cuts[phase + 1] - cuts[phase])
        k = (way * (n - 1) + step - 1) * phases + phase
        return pltpu.make_async_remote_copy(
            src_ref=leave.at[slot, piece], dst_ref=arrive.at[way, step - 1, piece],
            send_sem=sum_send.at[k], recv_sem=sum_recv.at[k],
            device_id={"tile": me + 1 - 2 * way}, device_id_type=mesh_ids)

    def sum_step(phase, i, way, step):
        size = cuts[phase + 1] - cuts[phase]
        piece = pl.ds(cuts[phase], size)
        slot = step - 1 if i < 2 else i
        if i:
            hop(way, step, phase, slot).wait_recv()
            value = (leave[slot, piece, :].astype(jnp.float32)
                     + arrive[way, step - 1, piece, :].astype(jnp.float32))
            leave[slot, piece, :] = value.astype(jnp.bfloat16)
        hop(way, step, phase, slot).start()

    def sums(phase, i):
        way = toward if i < 2 else 1 - toward

        def run(step, carry):
            sum_step(phase, i, way, step)
            return carry

        lax.fori_loop(1, n - i, run, 0)

    def ends(phase):
        @pl.when(is_end)
        def _():
            sums(phase, 0)

    def middle(phase, i):
        @pl.when(jnp.logical_not(is_end))
        def _():
            sums(phase, i)

    from_left = jnp.minimum(n - me, n - 1)
    from_right = jnp.minimum(me + 1, n - 1)

    def collect(phase):
        size = cuts[phase + 1] - cuts[phase]
        column = lax.broadcasted_iota(jnp.int32, (rows, size), 1) + cuts[phase]
        for way, there, step in ((0, me > 0, from_left), (1, me < n - 1, from_right)):
            @pl.when(there)
            def _():
                hop(way, step, phase, 0).wait_recv()

                back = jnp.where(column == ranks[:, :1], 1.0, 0.0).astype(jnp.bfloat16)
                own[...] += jnp.dot(
                    back, arrive[way, step - 1, pl.ds(cuts[phase], size), :], preferred_element_type=jnp.float32)

    def weigh(first, upto):
        def run(c, carry):
            at = pl.ds(pl.multiple_of(c * width, width), width)
            both = jnp.dot(turned[...], held[:, at], preferred_element_type=jnp.float32)
            weight_ref[:, at] = both[:hidden]
            bias_ref[:, at] = both[hidden:hidden + 1]
            return carry

        lax.fori_loop(first, upto, run, 0)

    m0.wait_recv()
    m1.wait_recv()
    use((t, 0), (t, 1), (mate, 0), (mate, 1))

    x0.wait_recv()
    yf = pass_on(xn, 0, yn)
    mx0 = pass_on(xn, 0, mate)
    y0.wait_recv()
    xf = pass_on(yn, 1, xn)
    my0 = pass_on(yn, 1, mate)
    mx0.wait_recv()
    my0.wait_recv()
    use((xn, 0), (yn, 1), (xn + across, 0), (yn + across, 1))
    pick_sums(0)
    ends(0)

    reorder(me, True)
    act_next(1)
    reorder_come(1)

    x1.wait_recv()
    mx1 = pass_on(xn, 1, mate)
    y1.wait_recv()
    my1 = pass_on(yn, 0, mate)
    mx1.wait_recv()
    my1.wait_recv()
    use((xn, 1), (yn, 0), (xn + across, 1), (yn + across, 0))
    pick_sums(1)
    ends(1)
    middle(0, 1)
    act_next(2)
    reorder_come(2)

    yf.wait_recv()
    md0 = pass_on(diag, 0, mate)
    xf.wait_recv()
    md1 = pass_on(diag, 1, mate)
    md0.wait_recv()
    md1.wait_recv()
    use((diag, 0), (diag, 1), (diag + across, 0), (diag + across, 1))
    pick_sums(2)
    ends(2)
    middle(0, 2)
    middle(1, 1)
    own[...] = chosen(spots, [me * rows], rows)
    middle(1, 2)
    act_next(3)
    reorder_come(3)
    blocks = columns // width
    weigh(0, blocks // 4)
    middle(2, 1)
    weigh(blocks // 4, blocks // 2)
    middle(2, 2)
    collect(0)
    collect(1)
    weigh(blocks // 2, blocks)
    collect(2)

    def finish(c, carry):
        at = pl.ds(pl.multiple_of(c * lanes, lanes), lanes)
        grad_ref[at, :] = own[at, :] * grad_ref[at, :]
        return carry

    lax.fori_loop(0, groups, finish, 0)

    for copy in (x0, y0, x1, y1, m0, m1, yf, mx0, xf, my0, mx1, my1, md0, md1):
        copy.wait_send()
    for way in range(2):
        for step in range(1, n):
            @pl.when((place(way) >= step - 1) & (place(way) < n - 1))
            def _():
                act_hop(way, step).wait_send()

            @pl.when(place(way) < n - step)
            def _():
                for phase in range(phases):
                    hop(way, step, phase, 0).wait_send()


def fused(n, cuts, grad_seq, places, pre_act, w_out):
    rows, hidden = pre_act.shape
    slots = rows * n
    columns = grad_seq.shape[1]
    width = 512
    anywhere, vmem = pl.BlockSpec(memory_space=pltpu.HBM), pl.BlockSpec(memory_space=pltpu.VMEM)

    def kernel(*refs):
        fused_kernel(n, cuts, width, *refs)

    sums = 2 * (n - 1) * (len(cuts) - 1)
    return pl.pallas_call(
        kernel,
        out_shape=(jax.ShapeDtypeStruct((rows, hidden), jnp.float32),
                   jax.ShapeDtypeStruct((hidden, columns), jnp.float32),
                   jax.ShapeDtypeStruct((1, columns), jnp.float32)),
        in_specs=[anywhere, anywhere, anywhere, vmem],
        out_specs=(vmem, vmem, vmem),
        scratch_shapes=[
            pltpu.VMEM((slots, columns), jnp.bfloat16),
            pltpu.VMEM((hidden, columns), jnp.bfloat16),
            pltpu.VMEM((slots, hidden), jnp.bfloat16),
            pltpu.VMEM((rows, hidden), jnp.bfloat16),
            pltpu.VMEM((n, hidden, rows), jnp.bfloat16),
            pltpu.VMEM((hidden + 16, slots), jnp.bfloat16),
            pltpu.VMEM((rows, hidden), jnp.float32),
            pltpu.VMEM((slots, 128), jnp.int32),
            pltpu.VMEM((slots, 128), jnp.int32),
            pltpu.VMEM((rows, 128), jnp.int32),
            pltpu.VMEM((2, n - 1, rows, hidden), jnp.bfloat16),
            pltpu.VMEM((n - 1, rows, hidden), jnp.bfloat16),
            pltpu.SemaphoreType.DMA((14,)),
            pltpu.SemaphoreType.DMA((14,)),
            pltpu.SemaphoreType.DMA((2 * (n - 1),)),
            pltpu.SemaphoreType.DMA((2 * (n - 1),)),
            pltpu.SemaphoreType.DMA((sums,)),
            pltpu.SemaphoreType.DMA((sums,)),
            pltpu.SemaphoreType.DMA((4,)),
        ],
        compiler_params=pltpu.CompilerParams(
            collective_id=0, has_side_effects=True, vmem_limit_bytes=52 * 2**20),
    )(grad_seq, w_out, pre_act, places)


def arrival_order_fits(positions, n_tile, n_text, cuts):
    pieces = 2 * n_text
    size = positions.shape[0] // pieces
    piece = jnp.arange(pieces, dtype=jnp.int32)[:, None, None] * size
    tiles = positions.reshape(1, n_tile, -1)
    held = jnp.sum((tiles >= piece) & (tiles < piece + size), axis=2, dtype=jnp.int32)
    held = held.reshape(2, 2, 2, 2, n_tile).sum(axis=2)
    flip_x, flip_y = held[:, ::-1], held[::-1]
    soon = held.sum(axis=2) + flip_x[:, :, 0] + flip_y[:, :, 1]
    later = held.sum(axis=2) + flip_x.sum(axis=2) + flip_y.sum(axis=2)
    return jnp.all((soon >= cuts[1]) & (later >= cuts[2]))


def line_sum(term, me, n, rows):
    def mine(block):
        start = jnp.clip(block, 0, n - 1) * rows
        return lax.dynamic_slice_in_dim(term, start, rows, 0).astype(jnp.float32)

    total = mine(me)
    right = left = None
    for step in range(1, n):
        ahead = n - step
        out_right, out_left = mine(me + ahead), mine(me - ahead)
        if right is not None:
            out_right = out_right + right.astype(jnp.float32)
            out_left = out_left + left.astype(jnp.float32)
        hops = range(min(step, n - 1))
        right = lax.ppermute(out_right.astype(jnp.bfloat16), "tile", [(i, i + 1) for i in hops])
        left = lax.ppermute(out_left.astype(jnp.bfloat16), "tile", [(n - 1 - i, n - 2 - i) for i in hops])
    return total + right.astype(jnp.float32) + left.astype(jnp.float32)


def solution(mesh):
    n_tile, n_text = mesh.shape["tile"], mesh.shape["text"]

    def steady(grad_seq, positions, pre_act, w_out):
        t, me = lax.axis_index("text"), lax.axis_index("tile")
        grows, columns = grad_seq.shape
        rows, hidden = pre_act.shape
        slots = positions.shape[0]
        around_text = [(i, (i + 1) % n_text) for i in range(n_text)]
        around_tile = [(i, (i + 1) % n_tile) for i in range(n_tile)]

        def places(tile):
            return lax.dynamic_slice_in_dim(positions, tile * rows, rows)

        def gather(k, carry):
            block, whole, term = carry
            block = jnp.where(k == 0, grad_seq, lax.ppermute(block, "text", around_text))
            start = (t - k) % n_text * grows
            part = jnp.einsum("so,ho->sh", block, w_out, preferred_element_type=jnp.float32)
            whole = lax.dynamic_update_slice_in_dim(whole, block, start, 0)
            term = lax.dynamic_update_slice_in_dim(term, part.astype(jnp.bfloat16), start, 0)
            return block, whole, term

        _, whole, term = lax.fori_loop(0, n_text, gather, (
            jnp.zeros_like(grad_seq), jnp.zeros((slots, columns), jnp.bfloat16), jnp.zeros((slots, hidden), jnp.bfloat16)))

        def activate(k, carry):
            block, act = carry
            block = jnp.where(k == 0, pre_act, lax.ppermute(block, "tile", around_tile))
            value = gelu_parts(block)[0].astype(jnp.bfloat16)
            act = act.at[places((me - k) % n_tile)].set(value, mode="promise_in_bounds", unique_indices=True)
            return block, act

        _, act = lax.fori_loop(0, n_tile, activate, (
            jnp.zeros_like(pre_act), jnp.zeros((slots, hidden), jnp.bfloat16)))

        def add(k, total):
            total = lax.ppermute(total, "tile", around_tile)
            return total + rows_of(term, places((me - 1 - k) % n_tile)).astype(jnp.float32)

        total = lax.fori_loop(0, n_tile, add, jnp.zeros((rows, hidden), jnp.float32))
        weight_term = jnp.einsum("sh,so->ho", act, whole, preferred_element_type=jnp.float32)
        return total * gelu_parts(pre_act)[1], weight_term, jnp.sum(whole, axis=0, dtype=jnp.float32)

    def plain(grad_seq, positions, pre_act, w_out):
        local_rows, hidden = pre_act.shape
        slots = positions.shape[0]
        me = lax.axis_index("tile")
        gathered = lax.all_gather(grad_seq, "text", axis=0, tiled=True)
        term = jnp.einsum(
            "so,ho->sh", gathered, w_out, preferred_element_type=jnp.float32).astype(jnp.bfloat16)

        blocks = [pre_act]
        for shift in range(1, n_tile):
            ring = [(i, (i + shift) % n_tile) for i in range(n_tile)]
            blocks.append(lax.ppermute(pre_act, "tile", ring))
        blocks = lax.optimization_barrier((blocks, term))[0]
        slot = jnp.arange(slots, dtype=jnp.int32)
        turned = (me - slot // local_rows) % n_tile * local_rows + slot % local_rows
        source = jnp.zeros((slots,), jnp.int32).at[positions].set(
            turned, mode="promise_in_bounds", unique_indices=True)
        act = jnp.concatenate([gelu_parts(b)[0].astype(jnp.bfloat16) for b in blocks], axis=0)
        act_seq = rows_of(act, source)
        slope = gelu_parts(pre_act)[1]

        cut = hidden // 2 // 128 * 128
        spans = [(0, cut), (cut, hidden)] if cut else [(0, hidden)]
        summed = []
        for lo, hi in spans:
            summed.append(line_sum(rows_of(term[:, lo:hi], positions), me, n_tile, local_rows))
        weight_term = jnp.einsum("sh,so->ho", act_seq, gathered, preferred_element_type=jnp.float32)
        local_sum = jnp.sum(gathered, axis=0, dtype=jnp.float32)
        grad_pre = jnp.concatenate(summed, axis=1) * slope
        return (grad_pre, weight_term, local_sum)

    def body(grad_seq, positions, pre_act, w_out):
        if n_tile != 4 or n_text != 8:
            return plain(grad_seq, positions, pre_act, w_out)
        rows = pre_act.shape[0]
        cuts = (0, rows * 2 // 5 // 16 * 16, rows * 27 // 40 // 16 * 16, rows)

        def quick(grad_seq, positions, pre_act, w_out):
            grad_pre, weight_term, bias = fused(n_tile, cuts, grad_seq, positions.reshape(-1, 128), pre_act, w_out)
            return (grad_pre, weight_term, bias.reshape(-1))

        fits = arrival_order_fits(positions, n_tile, n_text, cuts)
        return lax.cond(fits, quick, steady, grad_seq, positions, pre_act, w_out)

    in_specs = (P("text", "tile"), P(), P("tile", "text"), P("text", "tile"))
    out_specs = (P("tile", "text"), P("text", "tile"), P("tile"))
    return jax.shard_map(body, mesh=mesh, in_specs=in_specs, out_specs=out_specs, check_vma=False)
```

```python
import jax
import jax.numpy as jnp
from jax import lax
from jax.experimental import pallas as pl
from jax.experimental.pallas import tpu as pltpu
from jax.sharding import PartitionSpec as P


def gelu_parts(pre):
    value = pre.astype(jnp.float32)
    cdf = 0.5 * (1.0 + jax.scipy.special.erf(value * 0.7071067811865476))
    activated = value * cdf
    slope = cdf + value * jnp.exp(-0.5 * value * value) * 0.3989422804014327
    return (activated, slope)


def rows_of(table, index):
    return table.at[index].get(mode="promise_in_bounds", unique_indices=True)


def fused_kernel(n, cuts, width, early, g_ref, w_ref, pre_ref, place_ref, grad_ref, weight_ref, bias_ref,
                 held, weight, term, pre, act, turned, own, spots, packs, ranks, arrive, leave,
                 send_sem, recv_sem, act_send, act_recv, sum_send, sum_recv, own_sem):
    t, me = lax.axis_index("text"), lax.axis_index("tile")
    core, x, y = t % 2, t // 2 % 2, t // 4
    across, beside, above = 1 - 2 * core, 2 - 4 * x, 4 - 8 * y
    mate, xn, yn = t + across, t + beside, t + above
    diag = t + beside + above
    mesh_ids = pl.DeviceIdType.MESH
    grows = g_ref.shape[0]
    half = grows // 2
    rows, hidden = pre_ref.shape
    slots, columns = held.shape
    lanes = 128
    groups = rows // lanes
    phases = len(cuts) - 1

    loads = [pltpu.make_async_copy(pre_ref, pre, own_sem.at[0]), pltpu.make_async_copy(w_ref, weight, own_sem.at[1])]
    for copy in loads:
        copy.start()
    barrier = pltpu.get_barrier_semaphore()
    for other in (mate, xn, yn):
        pl.semaphore_signal(barrier, inc=1, device_id={"text": other}, device_id_type=mesh_ids)
    for other in ((me + 1) % n, (me + n - 1) % n):
        pl.semaphore_signal(barrier, inc=1, device_id={"tile": other}, device_id_type=mesh_ids)
    pl.semaphore_wait(barrier, 5)

    def part(owner, k):
        return pl.ds(pl.multiple_of(owner * grows + k * half, 16), half)

    count = [0]

    def send(src, dst, other):
        k = count[0]
        count[0] += 1
        copy = pltpu.make_async_remote_copy(
            src_ref=src, dst_ref=held.at[dst], send_sem=send_sem.at[k], recv_sem=recv_sem.at[k],
            device_id={"text": other}, device_id_type=mesh_ids)
        copy.start()
        return copy

    def mine(k):
        return g_ref.at[pl.ds(k * half, half)]

    def pass_on(owner, k, other):
        return send(held.at[part(owner, k)], part(owner, k), other)

    def use(*parts):
        spans = [part(owner, k) for owner, k in parts]
        value = lax.dot_general(
            jnp.concatenate([held[at, :] for at in spans], axis=0), weight[...], (((1,), (1,)), ((), ())),
            preferred_element_type=jnp.float32).astype(term.dtype)
        for c, at in enumerate(spans):
            term[at, :] = value[c * half:(c + 1) * half]

    def place(way):
        return me if way == 0 else n - 1 - me

    def act_copy(way, step, block):
        k = way * (n - 1) + step - 1
        return pltpu.make_async_remote_copy(
            src_ref=act.at[block], dst_ref=act.at[block], send_sem=act_send.at[k], recv_sem=act_recv.at[k],
            device_id={"tile": me + 1 - 2 * way}, device_id_type=mesh_ids)

    def act_hop(way, step):
        return act_copy(way, step, me - step + 1 if way == 0 else me + step - 1)

    def act_come(way, step):
        return act_copy(way, step, me - step if way == 0 else me + step)

    def act_next(step):
        for way in range(2):
            i = place(way)

            @pl.when(i >= step)
            def _():
                act_come(way, step).wait_recv()

                @pl.when(i < n - 1)
                def _():
                    act_hop(way, step + 1).start()

    def reorder(block, first):
        def run(c, carry):
            start = pl.multiple_of(c * width, width)
            column = lax.broadcasted_iota(jnp.int32, (rows, width), 1) + start
            at = pl.ds(pl.multiple_of(block * rows, lanes), rows)
            pick = jnp.where(column == spots[at, :][:, :1], 1.0, 0.0).astype(jnp.bfloat16)
            moved = jnp.dot(act[block], pick, preferred_element_type=jnp.float32)
            to = (pl.ds(0, hidden), pl.ds(start, width))
            if not first:
                moved = moved + turned[to].astype(jnp.float32)
            turned[to] = moved.astype(jnp.bfloat16)
            return carry

        lax.fori_loop(0, slots // width, run, 0)

    def reorder_come(step):
        def run(way, carry):
            i = me + way * (n - 1 - 2 * me)

            @pl.when(i >= step)
            def _():
                reorder(me - step + 2 * step * way, False)
            return carry

        lax.fori_loop(0, 2, run, 0)

    x0 = send(mine(0), part(t, 0), xn)
    y0 = send(mine(1), part(t, 1), yn)
    x1 = send(mine(1), part(t, 1), xn)
    y1 = send(mine(0), part(t, 0), yn)
    m0 = send(mine(0), part(t, 0), mate)
    m1 = send(mine(1), part(t, 1), mate)
    keep = [pltpu.make_async_copy(mine(k), held.at[part(t, k)], own_sem.at[2 + k]) for k in range(2)]
    for copy in keep:
        copy.start()

    loads[0].wait()

    def activate(c, carry):
        at = pl.ds(pl.multiple_of(c * lanes, lanes), lanes)
        activated, slope = gelu_parts(pre[at, :])
        grad_ref[at, :] = slope
        act[me, :, at] = activated.T.astype(jnp.bfloat16)
        return carry

    lax.fori_loop(0, groups, activate, 0)
    for way in range(2):
        @pl.when(place(way) < n - 1)
        def _():
            act_hop(way, 1).start()

    def clear(c, carry):
        term[pl.ds(pl.multiple_of(c * half, 16), half), :] = jnp.zeros((half, hidden), jnp.bfloat16)
        return carry

    lax.fori_loop(0, slots // half, clear, 0)
    turned[pl.ds(hidden, 16), :] = jnp.ones((16, slots), jnp.bfloat16)

    loads[1].wait()
    for k in range(2):
        keep[k].wait()

    def column_of(row):
        return jnp.broadcast_to(row, (lanes, lanes)).T

    earlier = jnp.where(
        lax.broadcasted_iota(jnp.int32, (rows, rows), 0) < lax.broadcasted_iota(jnp.int32, (rows, rows), 1),
        1.0, 0.0).astype(jnp.bfloat16)

    def rank_tile(d, carry):
        pieces = [place_ref[pl.ds(d * groups + g, 1), :] for g in range(groups)]
        row = jnp.concatenate(pieces, axis=1)

        def among(start, size):
            return jnp.where((row >= start) & (row < start + size), 1.0, 0.0)

        soon = among((t - core) * grows, 2 * grows)
        for owner, k in ((xn, 0), (yn, 1)):
            soon = soon + among(owner * grows + k * half, half) + among((owner + across) * grows + k * half, half)
        later = (among((xn - core) * grows, 2 * grows) + among((yn - core) * grows, 2 * grows)
                 + among((t - core) * grows, 2 * grows) - soon)
        late = 1.0 - soon - later
        kinds = jnp.concatenate([soon, later, late, jnp.zeros((13, rows), jnp.float32)], axis=0)
        before = jnp.dot(kinds.astype(jnp.bfloat16), earlier, preferred_element_type=jnp.float32)
        n_soon = jnp.sum(soon, axis=1, keepdims=True)
        n_later = jnp.sum(later, axis=1, keepdims=True)
        rank = (soon * before[0:1] + later * (before[1:2] + n_soon)
                + late * (before[2:3] + n_soon + n_later)).astype(jnp.int32)
        high = row >> 6
        parts = jnp.concatenate([high, row - (high << 6), jnp.zeros((14, rows), jnp.int32)], axis=0)
        parts = parts.astype(jnp.float32).astype(jnp.bfloat16)
        spread = lax.broadcasted_iota(jnp.int32, (lanes, rows), 1)
        total = jnp.zeros((16, rows), jnp.float32)
        for g in range(groups):
            span = slice(g * lanes, (g + 1) * lanes)
            column = column_of(rank[:, span])

            @pl.when(d == me)
            def _():
                ranks[span, :] = column
            pick = jnp.where(spread == column[:, :1], 1.0, 0.0).astype(jnp.bfloat16)
            total = total + jnp.dot(parts[:, span], pick, preferred_element_type=jnp.float32)
        packed = (total[0:1] * 64.0 + total[1:2]).astype(jnp.int32)
        for g in range(groups):
            span = slice(g * lanes, (g + 1) * lanes)
            at = pl.ds(pl.multiple_of(d * rows + g * lanes, lanes), lanes)
            packs[at, :] = column_of(packed[:, span])
            spots[at, :] = column_of(pieces[g])
        return carry

    lax.fori_loop(0, n, rank_tile, 0)

    is_end = (me == 0) | (me == n - 1)
    toward = jnp.where(me * 2 < n, 0, 1)

    def chosen(table, starts, size):
        spans = [pl.ds(pl.multiple_of(start, 16), size) for start in starts]
        column = lax.broadcasted_iota(jnp.int32, (size, slots), 1)
        picks = [jnp.where(column == table[at, :][:, :1], 1.0, 0.0).astype(jnp.bfloat16) for at in spans]
        pick = jnp.concatenate(picks, axis=0) if len(picks) > 1 else picks[0]
        return jnp.dot(pick, term[...], preferred_element_type=jnp.float32)

    def pick_sums(phase):
        size = cuts[phase + 1] - cuts[phase]
        tiles = []
        for slot in range(n - 1):
            first = (1 - toward) * (n - 1 - slot) + toward * slot
            tiles.append(first if slot < n - 2 else jnp.where(is_end, first, toward * (n - 1)))
        value = chosen(packs, [tile * rows + cuts[phase] for tile in tiles], size).astype(jnp.bfloat16)
        for slot in range(n - 1):
            leave[slot, pl.ds(cuts[phase], size), :] = value[slot * size:(slot + 1) * size]

    def hop(way, step, phase, slot):
        piece = pl.ds(cuts[phase], cuts[phase + 1] - cuts[phase])
        k = (way * (n - 1) + step - 1) * phases + phase
        return pltpu.make_async_remote_copy(
            src_ref=leave.at[slot, piece], dst_ref=arrive.at[way, step - 1, piece],
            send_sem=sum_send.at[k], recv_sem=sum_recv.at[k],
            device_id={"tile": me + 1 - 2 * way}, device_id_type=mesh_ids)

    def sum_step(phase, i, way, step):
        size = cuts[phase + 1] - cuts[phase]
        piece = pl.ds(cuts[phase], size)
        slot = step - 1 if i < 2 else i
        if i:
            hop(way, step, phase, slot).wait_recv()
            value = (leave[slot, piece, :].astype(jnp.float32)
                     + arrive[way, step - 1, piece, :].astype(jnp.float32))
            leave[slot, piece, :] = value.astype(jnp.bfloat16)
        hop(way, step, phase, slot).start()

    def sums(phase, i):
        way = toward if i < 2 else 1 - toward

        def run(step, carry):
            sum_step(phase, i, way, step)
            return carry

        lax.fori_loop(1, n - i, run, 0)

    def ends(phase):
        @pl.when(is_end)
        def _():
            sums(phase, 0)

    def middle(phase, i):
        @pl.when(jnp.logical_not(is_end))
        def _():
            sums(phase, i)

    from_left = jnp.minimum(n - me, n - 1)
    from_right = jnp.minimum(me + 1, n - 1)

    def collect(phase):
        size = cuts[phase + 1] - cuts[phase]
        column = lax.broadcasted_iota(jnp.int32, (rows, size), 1) + cuts[phase]
        for way, there, step in ((0, me > 0, from_left), (1, me < n - 1, from_right)):
            @pl.when(there)
            def _():
                hop(way, step, phase, 0).wait_recv()

                back = jnp.where(column == ranks[:, :1], 1.0, 0.0).astype(jnp.bfloat16)
                own[...] += jnp.dot(
                    back, arrive[way, step - 1, pl.ds(cuts[phase], size), :], preferred_element_type=jnp.float32)

    def weigh(first, upto):
        def run(c, carry):
            at = pl.ds(pl.multiple_of(c * width, width), width)
            both = jnp.dot(turned[...], held[:, at], preferred_element_type=jnp.float32)
            weight_ref[:, at] = both[:hidden]
            bias_ref[:, at] = both[hidden:hidden + 1]
            return carry

        lax.fori_loop(first, upto, run, 0)

    m0.wait_recv()
    m1.wait_recv()
    use((t, 0), (t, 1), (mate, 0), (mate, 1))

    x0.wait_recv()
    yf = pass_on(xn, 0, yn)
    mx0 = pass_on(xn, 0, mate)
    y0.wait_recv()
    xf = pass_on(yn, 1, xn)
    my0 = pass_on(yn, 1, mate)
    mx0.wait_recv()
    my0.wait_recv()
    use((xn, 0), (yn, 1), (xn + across, 0), (yn + across, 1))
    if early:
        pick_sums(0)
        ends(0)

    reorder(me, True)
    act_next(1)
    reorder_come(1)

    x1.wait_recv()
    mx1 = pass_on(xn, 1, mate)
    y1.wait_recv()
    my1 = pass_on(yn, 0, mate)
    mx1.wait_recv()
    my1.wait_recv()
    use((xn, 1), (yn, 0), (xn + across, 1), (yn + across, 0))
    if early:
        pick_sums(1)
        ends(1)
        middle(0, 1)
    act_next(2)
    reorder_come(2)

    yf.wait_recv()
    md0 = pass_on(diag, 0, mate)
    xf.wait_recv()
    md1 = pass_on(diag, 1, mate)
    md0.wait_recv()
    md1.wait_recv()
    use((diag, 0), (diag, 1), (diag + across, 0), (diag + across, 1))
    for phase in range(phases - 1 if early else 0, phases):
        pick_sums(phase)
        ends(phase)
    if not early:
        middle(0, 1)
    middle(0, 2)
    middle(1, 1)
    own[...] = chosen(spots, [me * rows], rows)
    middle(1, 2)
    act_next(3)
    reorder_come(3)
    blocks = columns // width
    weigh(0, blocks // 4)
    middle(2, 1)
    weigh(blocks // 4, blocks // 2)
    middle(2, 2)
    collect(0)
    collect(1)
    weigh(blocks // 2, blocks)
    collect(2)

    def finish(c, carry):
        at = pl.ds(pl.multiple_of(c * lanes, lanes), lanes)
        grad_ref[at, :] = own[at, :] * grad_ref[at, :]
        return carry

    lax.fori_loop(0, groups, finish, 0)

    for copy in (x0, y0, x1, y1, m0, m1, yf, mx0, xf, my0, mx1, my1, md0, md1):
        copy.wait_send()
    for way in range(2):
        for step in range(1, n):
            @pl.when((place(way) >= step - 1) & (place(way) < n - 1))
            def _():
                act_hop(way, step).wait_send()

            @pl.when(place(way) < n - step)
            def _():
                for phase in range(phases):
                    hop(way, step, phase, 0).wait_send()


def fused(n, cuts, early, grad_seq, places, pre_act, w_out):
    rows, hidden = pre_act.shape
    slots = rows * n
    columns = grad_seq.shape[1]
    width = 512
    anywhere, vmem = pl.BlockSpec(memory_space=pltpu.HBM), pl.BlockSpec(memory_space=pltpu.VMEM)

    def kernel(*refs):
        fused_kernel(n, cuts, width, early, *refs)

    sums = 2 * (n - 1) * (len(cuts) - 1)
    return pl.pallas_call(
        kernel,
        out_shape=(pltpu.VMEM((rows, hidden), jnp.float32),
                   pltpu.VMEM((hidden, columns), jnp.float32),
                   pltpu.VMEM((1, columns), jnp.float32)),
        in_specs=[anywhere, anywhere, anywhere, vmem],
        out_specs=(vmem, vmem, vmem),
        scratch_shapes=[
            pltpu.VMEM((slots, columns), jnp.bfloat16),
            pltpu.VMEM((hidden, columns), jnp.bfloat16),
            pltpu.VMEM((slots, hidden), jnp.bfloat16),
            pltpu.VMEM((rows, hidden), jnp.bfloat16),
            pltpu.VMEM((n, hidden, rows), jnp.bfloat16),
            pltpu.VMEM((hidden + 16, slots), jnp.bfloat16),
            pltpu.VMEM((rows, hidden), jnp.float32),
            pltpu.VMEM((slots, 128), jnp.int32),
            pltpu.VMEM((slots, 128), jnp.int32),
            pltpu.VMEM((rows, 128), jnp.int32),
            pltpu.VMEM((2, n - 1, rows, hidden), jnp.bfloat16),
            pltpu.VMEM((n - 1, rows, hidden), jnp.bfloat16),
            pltpu.SemaphoreType.DMA((14,)),
            pltpu.SemaphoreType.DMA((14,)),
            pltpu.SemaphoreType.DMA((2 * (n - 1),)),
            pltpu.SemaphoreType.DMA((2 * (n - 1),)),
            pltpu.SemaphoreType.DMA((sums,)),
            pltpu.SemaphoreType.DMA((sums,)),
            pltpu.SemaphoreType.DMA((4,)),
        ],
        compiler_params=pltpu.CompilerParams(
            collective_id=0 if early else 1, has_side_effects=True, vmem_limit_bytes=52 * 2**20),
    )(grad_seq, w_out, pre_act, places)


def arrival_order_fits(positions, n_tile, n_text, cuts):
    chip_rows = positions.shape[0] * 2 // n_text
    half = chip_rows // 4
    places = positions.reshape(1, n_tile, -1)
    chip = jnp.arange(n_text // 2, dtype=jnp.int32)[:, None, None]
    away = (places // chip_rows) ^ chip
    odd = places // half % 2
    soon = (away == 0) | (away == 1 + odd)
    later = away != 3
    counts = jnp.sum(soon.astype(jnp.int32) + later * 32768, axis=2)
    return jnp.all((counts % 32768 >= cuts[1]) & (counts // 32768 >= cuts[2]))


def line_sum(term, me, n, rows):
    def mine(block):
        start = jnp.clip(block, 0, n - 1) * rows
        return lax.dynamic_slice_in_dim(term, start, rows, 0).astype(jnp.float32)

    total = mine(me)
    right = left = None
    for step in range(1, n):
        ahead = n - step
        out_right, out_left = mine(me + ahead), mine(me - ahead)
        if right is not None:
            out_right = out_right + right.astype(jnp.float32)
            out_left = out_left + left.astype(jnp.float32)
        hops = range(min(step, n - 1))
        right = lax.ppermute(out_right.astype(jnp.bfloat16), "tile", [(i, i + 1) for i in hops])
        left = lax.ppermute(out_left.astype(jnp.bfloat16), "tile", [(n - 1 - i, n - 2 - i) for i in hops])
    return total + right.astype(jnp.float32) + left.astype(jnp.float32)


def solution(mesh):
    n_tile, n_text = mesh.shape["tile"], mesh.shape["text"]

    def plain(grad_seq, positions, pre_act, w_out):
        local_rows, hidden = pre_act.shape
        slots = positions.shape[0]
        me = lax.axis_index("tile")
        gathered = lax.all_gather(grad_seq, "text", axis=0, tiled=True)
        term = jnp.einsum(
            "so,ho->sh", gathered, w_out, preferred_element_type=jnp.float32).astype(jnp.bfloat16)

        blocks = [pre_act]
        for shift in range(1, n_tile):
            ring = [(i, (i + shift) % n_tile) for i in range(n_tile)]
            blocks.append(lax.ppermute(pre_act, "tile", ring))
        blocks = lax.optimization_barrier((blocks, term))[0]
        slot = jnp.arange(slots, dtype=jnp.int32)
        turned = (me - slot // local_rows) % n_tile * local_rows + slot % local_rows
        source = jnp.zeros((slots,), jnp.int32).at[positions].set(
            turned, mode="promise_in_bounds", unique_indices=True)
        act = jnp.concatenate([gelu_parts(b)[0].astype(jnp.bfloat16) for b in blocks], axis=0)
        act_seq = rows_of(act, source)
        slope = gelu_parts(pre_act)[1]

        cut = hidden // 2 // 128 * 128
        spans = [(0, cut), (cut, hidden)] if cut else [(0, hidden)]
        summed = []
        for lo, hi in spans:
            summed.append(line_sum(rows_of(term[:, lo:hi], positions), me, n_tile, local_rows))
        weight_term = jnp.einsum("sh,so->ho", act_seq, gathered, preferred_element_type=jnp.float32)
        local_sum = jnp.sum(gathered, axis=0, dtype=jnp.float32)
        grad_pre = jnp.concatenate(summed, axis=1) * slope
        return (grad_pre, weight_term, local_sum)

    def body(grad_seq, positions, pre_act, w_out):
        if n_tile != 4 or n_text != 8:
            return plain(grad_seq, positions, pre_act, w_out)
        rows = pre_act.shape[0]
        cuts = (0, rows * 2 // 5 // 16 * 16, rows * 27 // 40 // 16 * 16, rows)

        def run(early):
            def call(grad_seq, positions, pre_act, w_out):
                grad_pre, weight_term, bias = fused(
                    n_tile, cuts, early, grad_seq, positions.reshape(-1, 128), pre_act, w_out)
                return (grad_pre, weight_term, bias.reshape(-1))
            return call

        fits = arrival_order_fits(positions, n_tile, n_text, cuts)
        return lax.cond(fits, run(True), run(False), grad_seq, positions, pre_act, w_out)

    in_specs = (P("text", "tile"), P(), P("tile", "text"), P("text", "tile"))
    out_specs = (P("tile", "text"), P("text", "tile"), P("tile"))
    return jax.shard_map(body, mesh=mesh, in_specs=in_specs, out_specs=out_specs, check_vma=False)
```

```python
import jax
import jax.numpy as jnp
from jax import lax
from jax.experimental import pallas as pl
from jax.experimental.pallas import tpu as pltpu
from jax.sharding import PartitionSpec as P


def gelu_parts(pre):
    value = pre.astype(jnp.float32)
    cdf = 0.5 * (1.0 + jax.scipy.special.erf(value * 0.7071067811865476))
    activated = value * cdf
    slope = cdf + value * jnp.exp(-0.5 * value * value) * 0.3989422804014327
    return (activated, slope)


def rows_of(table, index):
    return table.at[index].get(mode="promise_in_bounds", unique_indices=True)


def fused_kernel(n, cuts, width, g_ref, w_ref, pre_ref, place_ref, grad_ref, weight_ref, bias_ref,
                 held, weight, term, pre, act, turned, own, spots, packs, ranks, arrive, leave,
                 send_sem, recv_sem, act_send, act_recv, sum_send, sum_recv, own_sem):
    t, me = lax.axis_index("text"), lax.axis_index("tile")
    core, x, y = t % 2, t // 2 % 2, t // 4
    across, beside, above = 1 - 2 * core, 2 - 4 * x, 4 - 8 * y
    mate, xn, yn = t + across, t + beside, t + above
    diag = t + beside + above
    mesh_ids = pl.DeviceIdType.MESH
    grows = g_ref.shape[0]
    half = grows // 2
    rows, hidden = pre_ref.shape
    slots, columns = held.shape
    lanes = 128
    groups = rows // lanes
    phases = len(cuts) - 1

    loads = [pltpu.make_async_copy(pre_ref, pre, own_sem.at[0]), pltpu.make_async_copy(w_ref, weight, own_sem.at[1])]
    for copy in loads:
        copy.start()
    barrier = pltpu.get_barrier_semaphore()
    for other in (mate, xn, yn):
        pl.semaphore_signal(barrier, inc=1, device_id={"text": other}, device_id_type=mesh_ids)
    for other in ((me + 1) % n, (me + n - 1) % n):
        pl.semaphore_signal(barrier, inc=1, device_id={"tile": other}, device_id_type=mesh_ids)
    pl.semaphore_wait(barrier, 5)

    def part(owner, k):
        return pl.ds(pl.multiple_of(owner * grows + k * half, 16), half)

    count = [0]

    def send(src, dst, other):
        k = count[0]
        count[0] += 1
        copy = pltpu.make_async_remote_copy(
            src_ref=src, dst_ref=held.at[dst], send_sem=send_sem.at[k], recv_sem=recv_sem.at[k],
            device_id={"text": other}, device_id_type=mesh_ids)
        copy.start()
        return copy

    def mine(k):
        return g_ref.at[pl.ds(k * half, half)]

    def pass_on(owner, k, other):
        return send(held.at[part(owner, k)], part(owner, k), other)

    def use(*parts):
        spans = [part(owner, k) for owner, k in parts]
        value = lax.dot_general(
            jnp.concatenate([held[at, :] for at in spans], axis=0), weight[...], (((1,), (1,)), ((), ())),
            preferred_element_type=jnp.float32).astype(term.dtype)
        for c, at in enumerate(spans):
            term[at, :] = value[c * half:(c + 1) * half]

    def place(way):
        return me if way == 0 else n - 1 - me

    def act_copy(way, step, block):
        k = way * (n - 1) + step - 1
        return pltpu.make_async_remote_copy(
            src_ref=act.at[block], dst_ref=act.at[block], send_sem=act_send.at[k], recv_sem=act_recv.at[k],
            device_id={"tile": me + 1 - 2 * way}, device_id_type=mesh_ids)

    def act_hop(way, step):
        return act_copy(way, step, me - step + 1 if way == 0 else me + step - 1)

    def act_come(way, step):
        return act_copy(way, step, me - step if way == 0 else me + step)

    def act_next(step):
        for way in range(2):
            i = place(way)

            @pl.when(i >= step)
            def _():
                act_come(way, step).wait_recv()

                @pl.when(i < n - 1)
                def _():
                    act_hop(way, step + 1).start()

    def reorder(block, first):
        def run(c, carry):
            start = pl.multiple_of(c * width, width)
            column = lax.broadcasted_iota(jnp.int32, (rows, width), 1) + start
            at = pl.ds(pl.multiple_of(block * rows, lanes), rows)
            pick = jnp.where(column == spots[at, :][:, :1], 1.0, 0.0).astype(jnp.bfloat16)
            moved = jnp.dot(act[block], pick, preferred_element_type=jnp.float32)
            to = (pl.ds(0, hidden), pl.ds(start, width))
            if not first:
                moved = moved + turned[to].astype(jnp.float32)
            turned[to] = moved.astype(jnp.bfloat16)
            return carry

        lax.fori_loop(0, slots // width, run, 0)

    def reorder_come(step):
        def run(way, carry):
            i = me + way * (n - 1 - 2 * me)

            @pl.when(i >= step)
            def _():
                reorder(me - step + 2 * step * way, False)
            return carry

        lax.fori_loop(0, 2, run, 0)

    x0 = send(mine(0), part(t, 0), xn)
    y0 = send(mine(1), part(t, 1), yn)
    x1 = send(mine(1), part(t, 1), xn)
    y1 = send(mine(0), part(t, 0), yn)
    m0 = send(mine(0), part(t, 0), mate)
    m1 = send(mine(1), part(t, 1), mate)
    keep = [pltpu.make_async_copy(mine(k), held.at[part(t, k)], own_sem.at[2 + k]) for k in range(2)]
    for copy in keep:
        copy.start()

    loads[0].wait()

    def activate(c, carry):
        at = pl.ds(pl.multiple_of(c * lanes, lanes), lanes)
        activated, slope = gelu_parts(pre[at, :])
        grad_ref[at, :] = slope
        act[me, :, at] = activated.T.astype(jnp.bfloat16)
        return carry

    lax.fori_loop(0, groups, activate, 0)
    for way in range(2):
        @pl.when(place(way) < n - 1)
        def _():
            act_hop(way, 1).start()

    def clear(c, carry):
        term[pl.ds(pl.multiple_of(c * half, 16), half), :] = jnp.zeros((half, hidden), jnp.bfloat16)
        return carry

    lax.fori_loop(0, slots // half, clear, 0)
    turned[pl.ds(hidden, 16), :] = jnp.ones((16, slots), jnp.bfloat16)

    loads[1].wait()
    for k in range(2):
        keep[k].wait()

    def column_of(row):
        return jnp.broadcast_to(row, (lanes, lanes)).T

    earlier = jnp.where(
        lax.broadcasted_iota(jnp.int32, (rows, rows), 0) < lax.broadcasted_iota(jnp.int32, (rows, rows), 1),
        1.0, 0.0).astype(jnp.bfloat16)

    def rank_tile(d, carry):
        pieces = [place_ref[pl.ds(d * groups + g, 1), :] for g in range(groups)]
        row = jnp.concatenate(pieces, axis=1)

        def among(start, size):
            return jnp.where((row >= start) & (row < start + size), 1.0, 0.0)

        soon = among((t - core) * grows, 2 * grows)
        for owner, k in ((xn, 0), (yn, 1)):
            soon = soon + among(owner * grows + k * half, half) + among((owner + across) * grows + k * half, half)
        later = (among((xn - core) * grows, 2 * grows) + among((yn - core) * grows, 2 * grows)
                 + among((t - core) * grows, 2 * grows) - soon)
        late = 1.0 - soon - later
        kinds = jnp.concatenate([soon, later, late, jnp.zeros((13, rows), jnp.float32)], axis=0)
        before = jnp.dot(kinds.astype(jnp.bfloat16), earlier, preferred_element_type=jnp.float32)
        n_soon = jnp.sum(soon, axis=1, keepdims=True)
        n_later = jnp.sum(later, axis=1, keepdims=True)
        rank = (soon * before[0:1] + later * (before[1:2] + n_soon)
                + late * (before[2:3] + n_soon + n_later)).astype(jnp.int32)
        high = row >> 6
        parts = jnp.concatenate([high, row - (high << 6), jnp.zeros((14, rows), jnp.int32)], axis=0)
        parts = parts.astype(jnp.float32).astype(jnp.bfloat16)
        spread = lax.broadcasted_iota(jnp.int32, (lanes, rows), 1)
        total = jnp.zeros((16, rows), jnp.float32)
        for g in range(groups):
            span = slice(g * lanes, (g + 1) * lanes)
            column = column_of(rank[:, span])

            @pl.when(d == me)
            def _():
                ranks[span, :] = column
            pick = jnp.where(spread == column[:, :1], 1.0, 0.0).astype(jnp.bfloat16)
            total = total + jnp.dot(parts[:, span], pick, preferred_element_type=jnp.float32)
        packed = (total[0:1] * 64.0 + total[1:2]).astype(jnp.int32)
        for g in range(groups):
            span = slice(g * lanes, (g + 1) * lanes)
            at = pl.ds(pl.multiple_of(d * rows + g * lanes, lanes), lanes)
            packs[at, :] = column_of(packed[:, span])
            spots[at, :] = column_of(pieces[g])
        return carry

    lax.fori_loop(0, n, rank_tile, 0)

    is_end = (me == 0) | (me == n - 1)
    toward = jnp.where(me * 2 < n, 0, 1)

    def chosen(table, starts, size):
        spans = [pl.ds(pl.multiple_of(start, 16), size) for start in starts]
        column = lax.broadcasted_iota(jnp.int32, (size, slots), 1)
        picks = [jnp.where(column == table[at, :][:, :1], 1.0, 0.0).astype(jnp.bfloat16) for at in spans]
        pick = jnp.concatenate(picks, axis=0) if len(picks) > 1 else picks[0]
        return jnp.dot(pick, term[...], preferred_element_type=jnp.float32)

    def pick_sums(phase):
        size = cuts[phase + 1] - cuts[phase]
        tiles = []
        for slot in range(n - 1):
            first = (1 - toward) * (n - 1 - slot) + toward * slot
            tiles.append(first if slot < n - 2 else jnp.where(is_end, first, toward * (n - 1)))
        value = chosen(packs, [tile * rows + cuts[phase] for tile in tiles], size).astype(jnp.bfloat16)
        for slot in range(n - 1):
            leave[slot, pl.ds(cuts[phase], size), :] = value[slot * size:(slot + 1) * size]

    def hop(way, step, phase, slot):
        piece = pl.ds(cuts[phase], cuts[phase + 1] - cuts[phase])
        k = (way * (n - 1) + step - 1) * phases + phase
        return pltpu.make_async_remote_copy(
            src_ref=leave.at[slot, piece], dst_ref=arrive.at[way, step - 1, piece],
            send_sem=sum_send.at[k], recv_sem=sum_recv.at[k],
            device_id={"tile": me + 1 - 2 * way}, device_id_type=mesh_ids)

    def sum_step(phase, i, way, step):
        size = cuts[phase + 1] - cuts[phase]
        piece = pl.ds(cuts[phase], size)
        slot = step - 1 if i < 2 else i
        if i:
            hop(way, step, phase, slot).wait_recv()
            value = (leave[slot, piece, :].astype(jnp.float32)
                     + arrive[way, step - 1, piece, :].astype(jnp.float32))
            leave[slot, piece, :] = value.astype(jnp.bfloat16)
        hop(way, step, phase, slot).start()

    def sums(phase, i):
        way = toward if i < 2 else 1 - toward

        def run(step, carry):
            sum_step(phase, i, way, step)
            return carry

        lax.fori_loop(1, n - i, run, 0)

    def ends(phase):
        @pl.when(is_end)
        def _():
            sums(phase, 0)

    def middle(phase, i):
        @pl.when(jnp.logical_not(is_end))
        def _():
            sums(phase, i)

    from_left = jnp.minimum(n - me, n - 1)
    from_right = jnp.minimum(me + 1, n - 1)

    def collect(phase):
        size = cuts[phase + 1] - cuts[phase]
        column = lax.broadcasted_iota(jnp.int32, (rows, size), 1) + cuts[phase]
        for way, there, step in ((0, me > 0, from_left), (1, me < n - 1, from_right)):
            @pl.when(there)
            def _():
                hop(way, step, phase, 0).wait_recv()

                back = jnp.where(column == ranks[:, :1], 1.0, 0.0).astype(jnp.bfloat16)
                own[...] += jnp.dot(
                    back, arrive[way, step - 1, pl.ds(cuts[phase], size), :], preferred_element_type=jnp.float32)

    def weigh(first, upto):
        def run(c, carry):
            at = pl.ds(pl.multiple_of(c * width, width), width)
            both = jnp.dot(turned[...], held[:, at], preferred_element_type=jnp.float32)
            weight_ref[:, at] = both[:hidden]
            bias_ref[:, at] = both[hidden:hidden + 1]
            return carry

        lax.fori_loop(first, upto, run, 0)

    m0.wait_recv()
    m1.wait_recv()
    use((t, 0), (t, 1), (mate, 0), (mate, 1))

    x0.wait_recv()
    yf = pass_on(xn, 0, yn)
    mx0 = pass_on(xn, 0, mate)
    y0.wait_recv()
    xf = pass_on(yn, 1, xn)
    my0 = pass_on(yn, 1, mate)
    mx0.wait_recv()
    my0.wait_recv()
    use((xn, 0), (yn, 1), (xn + across, 0), (yn + across, 1))
    pick_sums(0)
    ends(0)

    reorder(me, True)
    act_next(1)
    reorder_come(1)

    x1.wait_recv()
    mx1 = pass_on(xn, 1, mate)
    y1.wait_recv()
    my1 = pass_on(yn, 0, mate)
    mx1.wait_recv()
    my1.wait_recv()
    use((xn, 1), (yn, 0), (xn + across, 1), (yn + across, 0))
    pick_sums(1)
    ends(1)
    middle(0, 1)
    act_next(2)
    reorder_come(2)

    yf.wait_recv()
    md0 = pass_on(diag, 0, mate)
    xf.wait_recv()
    md1 = pass_on(diag, 1, mate)
    md0.wait_recv()
    md1.wait_recv()
    use((diag, 0), (diag, 1), (diag + across, 0), (diag + across, 1))
    pick_sums(2)
    ends(2)
    middle(0, 2)
    middle(1, 1)
    own[...] = chosen(spots, [me * rows], rows)
    middle(1, 2)
    act_next(3)
    reorder_come(3)
    blocks = columns // width
    weigh(0, blocks // 4)
    middle(2, 1)
    weigh(blocks // 4, blocks // 2)
    middle(2, 2)
    collect(0)
    collect(1)
    weigh(blocks // 2, blocks)
    collect(2)

    def finish(c, carry):
        at = pl.ds(pl.multiple_of(c * lanes, lanes), lanes)
        grad_ref[at, :] = own[at, :] * grad_ref[at, :]
        return carry

    lax.fori_loop(0, groups, finish, 0)

    for copy in (x0, y0, x1, y1, m0, m1, yf, mx0, xf, my0, mx1, my1, md0, md1):
        copy.wait_send()
    for way in range(2):
        for step in range(1, n):
            @pl.when((place(way) >= step - 1) & (place(way) < n - 1))
            def _():
                act_hop(way, step).wait_send()

            @pl.when(place(way) < n - step)
            def _():
                for phase in range(phases):
                    hop(way, step, phase, 0).wait_send()


def fused(n, cuts, grad_seq, places, pre_act, w_out):
    rows, hidden = pre_act.shape
    slots = rows * n
    columns = grad_seq.shape[1]
    width = 512
    anywhere, vmem = pl.BlockSpec(memory_space=pltpu.HBM), pl.BlockSpec(memory_space=pltpu.VMEM)

    def kernel(*refs):
        fused_kernel(n, cuts, width, *refs)

    sums = 2 * (n - 1) * (len(cuts) - 1)
    return pl.pallas_call(
        kernel,
        out_shape=(pltpu.VMEM((rows, hidden), jnp.float32),
                   pltpu.VMEM((hidden, columns), jnp.float32),
                   pltpu.VMEM((1, columns), jnp.float32)),
        in_specs=[anywhere, anywhere, anywhere, vmem],
        out_specs=(vmem, vmem, vmem),
        scratch_shapes=[
            pltpu.VMEM((slots, columns), jnp.bfloat16),
            pltpu.VMEM((hidden, columns), jnp.bfloat16),
            pltpu.VMEM((slots, hidden), jnp.bfloat16),
            pltpu.VMEM((rows, hidden), jnp.bfloat16),
            pltpu.VMEM((n, hidden, rows), jnp.bfloat16),
            pltpu.VMEM((hidden + 16, slots), jnp.bfloat16),
            pltpu.VMEM((rows, hidden), jnp.float32),
            pltpu.VMEM((slots, 128), jnp.int32),
            pltpu.VMEM((slots, 128), jnp.int32),
            pltpu.VMEM((rows, 128), jnp.int32),
            pltpu.VMEM((2, n - 1, rows, hidden), jnp.bfloat16),
            pltpu.VMEM((n - 1, rows, hidden), jnp.bfloat16),
            pltpu.SemaphoreType.DMA((14,)),
            pltpu.SemaphoreType.DMA((14,)),
            pltpu.SemaphoreType.DMA((2 * (n - 1),)),
            pltpu.SemaphoreType.DMA((2 * (n - 1),)),
            pltpu.SemaphoreType.DMA((sums,)),
            pltpu.SemaphoreType.DMA((sums,)),
            pltpu.SemaphoreType.DMA((4,)),
        ],
        compiler_params=pltpu.CompilerParams(
            collective_id=0, has_side_effects=True, vmem_limit_bytes=52 * 2**20),
    )(grad_seq, w_out, pre_act, places)


def arrival_order_fits(positions, n_tile, n_text, cuts):
    chip_rows = positions.shape[0] * 2 // n_text
    half = chip_rows // 4
    places = positions.reshape(1, n_tile, -1)
    chip = jnp.arange(n_text // 2, dtype=jnp.int32)[:, None, None]
    away = (places // chip_rows) ^ chip
    odd = places // half % 2
    soon = (away == 0) | (away == 1 + odd)
    later = away != 3
    counts = jnp.sum(soon.astype(jnp.int32) + later * 32768, axis=2)
    return jnp.all((counts % 32768 >= cuts[1]) & (counts // 32768 >= cuts[2]))


def line_sum(term, me, n, rows):
    def mine(block):
        start = jnp.clip(block, 0, n - 1) * rows
        return lax.dynamic_slice_in_dim(term, start, rows, 0).astype(jnp.float32)

    total = mine(me)
    right = left = None
    for step in range(1, n):
        ahead = n - step
        out_right, out_left = mine(me + ahead), mine(me - ahead)
        if right is not None:
            out_right = out_right + right.astype(jnp.float32)
            out_left = out_left + left.astype(jnp.float32)
        hops = range(min(step, n - 1))
        right = lax.ppermute(out_right.astype(jnp.bfloat16), "tile", [(i, i + 1) for i in hops])
        left = lax.ppermute(out_left.astype(jnp.bfloat16), "tile", [(n - 1 - i, n - 2 - i) for i in hops])
    return total + right.astype(jnp.float32) + left.astype(jnp.float32)


def solution(mesh):
    n_tile, n_text = mesh.shape["tile"], mesh.shape["text"]

    def steady(grad_seq, positions, pre_act, w_out):
        t, me = lax.axis_index("text"), lax.axis_index("tile")
        grows, columns = grad_seq.shape
        rows, hidden = pre_act.shape
        slots = positions.shape[0]
        around_text = [(i, (i + 1) % n_text) for i in range(n_text)]
        around_tile = [(i, (i + 1) % n_tile) for i in range(n_tile)]

        def places(tile):
            return lax.dynamic_slice_in_dim(positions, tile * rows, rows)

        def gather(k, carry):
            block, whole, term = carry
            block = jnp.where(k == 0, grad_seq, lax.ppermute(block, "text", around_text))
            start = (t - k) % n_text * grows
            part = jnp.einsum("so,ho->sh", block, w_out, preferred_element_type=jnp.float32)
            whole = lax.dynamic_update_slice_in_dim(whole, block, start, 0)
            term = lax.dynamic_update_slice_in_dim(term, part.astype(jnp.bfloat16), start, 0)
            return block, whole, term

        _, whole, term = lax.fori_loop(0, n_text, gather, (
            jnp.zeros_like(grad_seq), jnp.zeros((slots, columns), jnp.bfloat16), jnp.zeros((slots, hidden), jnp.bfloat16)))

        def activate(k, carry):
            block, act = carry
            block = jnp.where(k == 0, pre_act, lax.ppermute(block, "tile", around_tile))
            value = gelu_parts(block)[0].astype(jnp.bfloat16)
            act = act.at[places((me - k) % n_tile)].set(value, mode="promise_in_bounds", unique_indices=True)
            return block, act

        _, act = lax.fori_loop(0, n_tile, activate, (
            jnp.zeros_like(pre_act), jnp.zeros((slots, hidden), jnp.bfloat16)))

        def add(k, total):
            total = lax.ppermute(total, "tile", around_tile)
            return total + rows_of(term, places((me - 1 - k) % n_tile)).astype(jnp.float32)

        total = lax.fori_loop(0, n_tile, add, jnp.zeros((rows, hidden), jnp.float32))
        weight_term = jnp.einsum("sh,so->ho", act, whole, preferred_element_type=jnp.float32)
        return total * gelu_parts(pre_act)[1], weight_term, jnp.sum(whole, axis=0, dtype=jnp.float32)

    def plain(grad_seq, positions, pre_act, w_out):
        local_rows, hidden = pre_act.shape
        slots = positions.shape[0]
        me = lax.axis_index("tile")
        gathered = lax.all_gather(grad_seq, "text", axis=0, tiled=True)
        term = jnp.einsum(
            "so,ho->sh", gathered, w_out, preferred_element_type=jnp.float32).astype(jnp.bfloat16)

        blocks = [pre_act]
        for shift in range(1, n_tile):
            ring = [(i, (i + shift) % n_tile) for i in range(n_tile)]
            blocks.append(lax.ppermute(pre_act, "tile", ring))
        blocks = lax.optimization_barrier((blocks, term))[0]
        slot = jnp.arange(slots, dtype=jnp.int32)
        turned = (me - slot // local_rows) % n_tile * local_rows + slot % local_rows
        source = jnp.zeros((slots,), jnp.int32).at[positions].set(
            turned, mode="promise_in_bounds", unique_indices=True)
        act = jnp.concatenate([gelu_parts(b)[0].astype(jnp.bfloat16) for b in blocks], axis=0)
        act_seq = rows_of(act, source)
        slope = gelu_parts(pre_act)[1]

        cut = hidden // 2 // 128 * 128
        spans = [(0, cut), (cut, hidden)] if cut else [(0, hidden)]
        summed = []
        for lo, hi in spans:
            summed.append(line_sum(rows_of(term[:, lo:hi], positions), me, n_tile, local_rows))
        weight_term = jnp.einsum("sh,so->ho", act_seq, gathered, preferred_element_type=jnp.float32)
        local_sum = jnp.sum(gathered, axis=0, dtype=jnp.float32)
        grad_pre = jnp.concatenate(summed, axis=1) * slope
        return (grad_pre, weight_term, local_sum)

    def body(grad_seq, positions, pre_act, w_out):
        if n_tile != 4 or n_text != 8:
            return plain(grad_seq, positions, pre_act, w_out)
        rows = pre_act.shape[0]
        cuts = (0, rows * 2 // 5 // 16 * 16, rows * 27 // 40 // 16 * 16, rows)

        def quick(grad_seq, positions, pre_act, w_out):
            grad_pre, weight_term, bias = fused(n_tile, cuts, grad_seq, positions.reshape(-1, 128), pre_act, w_out)
            return (grad_pre, weight_term, bias.reshape(-1))

        fits = arrival_order_fits(positions, n_tile, n_text, cuts)
        return lax.cond(fits, quick, steady, grad_seq, positions, pre_act, w_out)

    in_specs = (P("text", "tile"), P(), P("tile", "text"), P("text", "tile"))
    out_specs = (P("tile", "text"), P("text", "tile"), P("tile"))
    return jax.shard_map(body, mesh=mesh, in_specs=in_specs, out_specs=out_specs, check_vma=False)
```

```python
import jax
import jax.numpy as jnp
from jax import lax
from jax.experimental import pallas as pl
from jax.experimental.pallas import tpu as pltpu
from jax.sharding import PartitionSpec as P


def gelu_parts(pre):
    value = pre.astype(jnp.float32)
    cdf = 0.5 * (1.0 + jax.scipy.special.erf(value * 0.7071067811865476))
    activated = value * cdf
    slope = cdf + value * jnp.exp(-0.5 * value * value) * 0.3989422804014327
    return (activated, slope)


def rows_of(table, index):
    return table.at[index].get(mode="promise_in_bounds", unique_indices=True)


def fused_kernel(n, cuts, width, g_ref, w_ref, pre_ref, place_ref, grad_ref, weight_ref, bias_ref,
                 held, weight, term, pre, act, turned, own, spots, packs, ranks, arrive, leave,
                 send_sem, recv_sem, act_send, act_recv, sum_send, sum_recv, own_sem):
    t, me = lax.axis_index("text"), lax.axis_index("tile")
    core, x, y = t % 2, t // 2 % 2, t // 4
    across, beside, above = 1 - 2 * core, 2 - 4 * x, 4 - 8 * y
    mate, xn, yn = t + across, t + beside, t + above
    diag = t + beside + above
    mesh_ids = pl.DeviceIdType.MESH
    grows = g_ref.shape[0]
    half = grows // 2
    rows, hidden = pre_ref.shape
    slots, columns = held.shape
    lanes = 128
    groups = rows // lanes
    phases = len(cuts) - 1

    loads = [pltpu.make_async_copy(pre_ref, pre, own_sem.at[0]), pltpu.make_async_copy(w_ref, weight, own_sem.at[1])]
    for copy in loads:
        copy.start()
    barrier = pltpu.get_barrier_semaphore()
    for other in (mate, xn, yn):
        pl.semaphore_signal(barrier, inc=1, device_id={"text": other}, device_id_type=mesh_ids)
    for other in ((me + 1) % n, (me + n - 1) % n):
        pl.semaphore_signal(barrier, inc=1, device_id={"tile": other}, device_id_type=mesh_ids)
    pl.semaphore_wait(barrier, 5)

    def part(owner, k):
        return pl.ds(pl.multiple_of(owner * grows + k * half, 16), half)

    count = [0]

    def send(src, dst, other):
        k = count[0]
        count[0] += 1
        copy = pltpu.make_async_remote_copy(
            src_ref=src, dst_ref=held.at[dst], send_sem=send_sem.at[k], recv_sem=recv_sem.at[k],
            device_id={"text": other}, device_id_type=mesh_ids)
        copy.start()
        return copy

    def mine(k):
        return g_ref.at[pl.ds(k * half, half)]

    def pass_on(owner, k, other):
        return send(held.at[part(owner, k)], part(owner, k), other)

    def use(*parts):
        spans = [part(owner, k) for owner, k in parts]
        value = lax.dot_general(
            jnp.concatenate([held[at, :] for at in spans], axis=0), weight[...], (((1,), (1,)), ((), ())),
            preferred_element_type=jnp.float32).astype(term.dtype)
        for c, at in enumerate(spans):
            term[at, :] = value[c * half:(c + 1) * half]

    def place(way):
        return me if way == 0 else n - 1 - me

    def act_copy(way, step, block):
        k = way * (n - 1) + step - 1
        return pltpu.make_async_remote_copy(
            src_ref=act.at[block], dst_ref=act.at[block], send_sem=act_send.at[k], recv_sem=act_recv.at[k],
            device_id={"tile": me + 1 - 2 * way}, device_id_type=mesh_ids)

    def act_hop(way, step):
        return act_copy(way, step, me - step + 1 if way == 0 else me + step - 1)

    def act_come(way, step):
        return act_copy(way, step, me - step if way == 0 else me + step)

    def act_next(step):
        for way in range(2):
            i = place(way)

            @pl.when(i >= step)
            def _():
                act_come(way, step).wait_recv()

                @pl.when(i < n - 1)
                def _():
                    act_hop(way, step + 1).start()

    def reorder(block, first):
        def run(c, carry):
            start = pl.multiple_of(c * width, width)
            column = lax.broadcasted_iota(jnp.int32, (rows, width), 1) + start
            at = pl.ds(pl.multiple_of(block * rows, lanes), rows)
            pick = jnp.where(column == spots[at, :][:, :1], 1.0, 0.0).astype(jnp.bfloat16)
            moved = jnp.dot(act[block], pick, preferred_element_type=jnp.float32)
            to = (pl.ds(0, hidden), pl.ds(start, width))
            if not first:
                moved = moved + turned[to].astype(jnp.float32)
            turned[to] = moved.astype(jnp.bfloat16)
            return carry

        lax.fori_loop(0, slots // width, run, 0)

    def reorder_come(step):
        def run(way, carry):
            i = me + way * (n - 1 - 2 * me)

            @pl.when(i >= step)
            def _():
                reorder(me - step + 2 * step * way, False)
            return carry

        lax.fori_loop(0, 2, run, 0)

    x0 = send(mine(0), part(t, 0), xn)
    y0 = send(mine(1), part(t, 1), yn)
    x1 = send(mine(1), part(t, 1), xn)
    y1 = send(mine(0), part(t, 0), yn)
    m0 = send(mine(0), part(t, 0), mate)
    m1 = send(mine(1), part(t, 1), mate)
    keep = [pltpu.make_async_copy(mine(k), held.at[part(t, k)], own_sem.at[2 + k]) for k in range(2)]
    for copy in keep:
        copy.start()

    loads[0].wait()

    def activate(c, carry):
        at = pl.ds(pl.multiple_of(c * lanes, lanes), lanes)
        activated, slope = gelu_parts(pre[at, :])
        grad_ref[at, :] = slope
        act[me, :, at] = activated.T.astype(jnp.bfloat16)
        return carry

    lax.fori_loop(0, groups, activate, 0)
    for way in range(2):
        @pl.when(place(way) < n - 1)
        def _():
            act_hop(way, 1).start()

    def clear(c, carry):
        term[pl.ds(pl.multiple_of(c * half, 16), half), :] = jnp.zeros((half, hidden), jnp.bfloat16)
        return carry

    lax.fori_loop(0, slots // half, clear, 0)
    turned[pl.ds(hidden, 16), :] = jnp.ones((16, slots), jnp.bfloat16)

    loads[1].wait()
    for k in range(2):
        keep[k].wait()

    def column_of(row):
        return jnp.broadcast_to(row, (lanes, lanes)).T

    earlier = jnp.where(
        lax.broadcasted_iota(jnp.int32, (rows, rows), 0) < lax.broadcasted_iota(jnp.int32, (rows, rows), 1),
        1.0, 0.0).astype(jnp.bfloat16)

    def rank_tile(d, carry):
        pieces = [place_ref[pl.ds(d * groups + g, 1), :] for g in range(groups)]
        row = jnp.concatenate(pieces, axis=1)

        def among(start, size):
            return jnp.where((row >= start) & (row < start + size), 1.0, 0.0)

        soon = among((t - core) * grows, 2 * grows)
        for owner, k in ((xn, 0), (yn, 1)):
            soon = soon + among(owner * grows + k * half, half) + among((owner + across) * grows + k * half, half)
        later = (among((xn - core) * grows, 2 * grows) + among((yn - core) * grows, 2 * grows)
                 + among((t - core) * grows, 2 * grows) - soon)
        late = 1.0 - soon - later
        kinds = jnp.concatenate([soon, later, late, jnp.zeros((13, rows), jnp.float32)], axis=0)
        before = jnp.dot(kinds.astype(jnp.bfloat16), earlier, preferred_element_type=jnp.float32)
        n_soon = jnp.sum(soon, axis=1, keepdims=True)
        n_later = jnp.sum(later, axis=1, keepdims=True)
        rank = (soon * before[0:1] + later * (before[1:2] + n_soon)
                + late * (before[2:3] + n_soon + n_later)).astype(jnp.int32)
        high = row >> 6
        parts = jnp.concatenate([high, row - (high << 6), jnp.zeros((14, rows), jnp.int32)], axis=0)
        parts = parts.astype(jnp.float32).astype(jnp.bfloat16)
        spread = lax.broadcasted_iota(jnp.int32, (lanes, rows), 1)
        total = jnp.zeros((16, rows), jnp.float32)
        for g in range(groups):
            span = slice(g * lanes, (g + 1) * lanes)
            column = column_of(rank[:, span])

            @pl.when(d == me)
            def _():
                ranks[span, :] = column
            pick = jnp.where(spread == column[:, :1], 1.0, 0.0).astype(jnp.bfloat16)
            total = total + jnp.dot(parts[:, span], pick, preferred_element_type=jnp.float32)
        packed = (total[0:1] * 64.0 + total[1:2]).astype(jnp.int32)
        for g in range(groups):
            span = slice(g * lanes, (g + 1) * lanes)
            at = pl.ds(pl.multiple_of(d * rows + g * lanes, lanes), lanes)
            packs[at, :] = column_of(packed[:, span])
            spots[at, :] = column_of(pieces[g])
        return carry

    lax.fori_loop(0, n, rank_tile, 0)

    is_end = (me == 0) | (me == n - 1)
    toward = jnp.where(me * 2 < n, 0, 1)

    def chosen(table, starts, size):
        spans = [pl.ds(pl.multiple_of(start, 16), size) for start in starts]
        column = lax.broadcasted_iota(jnp.int32, (size, slots), 1)
        picks = [jnp.where(column == table[at, :][:, :1], 1.0, 0.0).astype(jnp.bfloat16) for at in spans]
        pick = jnp.concatenate(picks, axis=0) if len(picks) > 1 else picks[0]
        return jnp.dot(pick, term[...], preferred_element_type=jnp.float32)

    def pick_sums(phase):
        size = cuts[phase + 1] - cuts[phase]
        tiles = []
        for slot in range(n - 1):
            first = (1 - toward) * (n - 1 - slot) + toward * slot
            tiles.append(first if slot < n - 2 else jnp.where(is_end, first, toward * (n - 1)))
        value = chosen(packs, [tile * rows + cuts[phase] for tile in tiles], size).astype(jnp.bfloat16)
        for slot in range(n - 1):
            leave[slot, pl.ds(cuts[phase], size), :] = value[slot * size:(slot + 1) * size]

    def hop(way, step, phase, slot):
        piece = pl.ds(cuts[phase], cuts[phase + 1] - cuts[phase])
        k = (way * (n - 1) + step - 1) * phases + phase
        return pltpu.make_async_remote_copy(
            src_ref=leave.at[slot, piece], dst_ref=arrive.at[way, step - 1, piece],
            send_sem=sum_send.at[k], recv_sem=sum_recv.at[k],
            device_id={"tile": me + 1 - 2 * way}, device_id_type=mesh_ids)

    def sum_step(phase, i, way, step):
        size = cuts[phase + 1] - cuts[phase]
        piece = pl.ds(cuts[phase], size)
        slot = step - 1 if i < 2 else i
        if i:
            hop(way, step, phase, slot).wait_recv()
            value = (leave[slot, piece, :].astype(jnp.float32)
                     + arrive[way, step - 1, piece, :].astype(jnp.float32))
            leave[slot, piece, :] = value.astype(jnp.bfloat16)
        hop(way, step, phase, slot).start()

    def sums(phase, i):
        way = toward if i < 2 else 1 - toward

        def run(step, carry):
            sum_step(phase, i, way, step)
            return carry

        lax.fori_loop(1, n - i, run, 0)

    def ends(phase):
        @pl.when(is_end)
        def _():
            sums(phase, 0)

    def middle(phase, i):
        @pl.when(jnp.logical_not(is_end))
        def _():
            sums(phase, i)

    from_left = jnp.minimum(n - me, n - 1)
    from_right = jnp.minimum(me + 1, n - 1)

    def collect(phase):
        size = cuts[phase + 1] - cuts[phase]
        column = lax.broadcasted_iota(jnp.int32, (rows, size), 1) + cuts[phase]
        for way, there, step in ((0, me > 0, from_left), (1, me < n - 1, from_right)):
            @pl.when(there)
            def _():
                hop(way, step, phase, 0).wait_recv()

                back = jnp.where(column == ranks[:, :1], 1.0, 0.0).astype(jnp.bfloat16)
                own[...] += jnp.dot(
                    back, arrive[way, step - 1, pl.ds(cuts[phase], size), :], preferred_element_type=jnp.float32)

    def weigh(first, upto):
        def run(c, carry):
            at = pl.ds(pl.multiple_of(c * width, width), width)
            both = jnp.dot(turned[...], held[:, at], preferred_element_type=jnp.float32)
            weight_ref[:, at] = both[:hidden]
            bias_ref[:, at] = both[hidden:hidden + 1]
            return carry

        lax.fori_loop(first, upto, run, 0)

    m0.wait_recv()
    m1.wait_recv()
    use((t, 0), (t, 1), (mate, 0), (mate, 1))

    x0.wait_recv()
    yf = pass_on(xn, 0, yn)
    mx0 = pass_on(xn, 0, mate)
    y0.wait_recv()
    xf = pass_on(yn, 1, xn)
    my0 = pass_on(yn, 1, mate)
    mx0.wait_recv()
    my0.wait_recv()
    use((xn, 0), (yn, 1), (xn + across, 0), (yn + across, 1))
    pick_sums(0)
    ends(0)

    reorder(me, True)
    act_next(1)
    reorder_come(1)

    x1.wait_recv()
    mx1 = pass_on(xn, 1, mate)
    y1.wait_recv()
    my1 = pass_on(yn, 0, mate)
    mx1.wait_recv()
    my1.wait_recv()
    use((xn, 1), (yn, 0), (xn + across, 1), (yn + across, 0))
    pick_sums(1)
    ends(1)
    middle(0, 1)
    act_next(2)
    reorder_come(2)

    yf.wait_recv()
    md0 = pass_on(diag, 0, mate)
    xf.wait_recv()
    md1 = pass_on(diag, 1, mate)
    md0.wait_recv()
    md1.wait_recv()
    use((diag, 0), (diag, 1), (diag + across, 0), (diag + across, 1))
    pick_sums(2)
    ends(2)
    middle(0, 2)
    middle(1, 1)
    own[...] = chosen(spots, [me * rows], rows)
    middle(1, 2)
    act_next(3)
    reorder_come(3)
    blocks = columns // width
    weigh(0, blocks // 4)
    middle(2, 1)
    weigh(blocks // 4, blocks // 2)
    middle(2, 2)
    collect(0)
    collect(1)
    weigh(blocks // 2, blocks)
    collect(2)

    def finish(c, carry):
        at = pl.ds(pl.multiple_of(c * lanes, lanes), lanes)
        grad_ref[at, :] = own[at, :] * grad_ref[at, :]
        return carry

    lax.fori_loop(0, groups, finish, 0)

    for copy in (x0, y0, x1, y1, m0, m1, yf, mx0, xf, my0, mx1, my1, md0, md1):
        copy.wait_send()
    for way in range(2):
        for step in range(1, n):
            @pl.when((place(way) >= step - 1) & (place(way) < n - 1))
            def _():
                act_hop(way, step).wait_send()

            @pl.when(place(way) < n - step)
            def _():
                for phase in range(phases):
                    hop(way, step, phase, 0).wait_send()


def fused(n, cuts, grad_seq, places, pre_act, w_out):
    rows, hidden = pre_act.shape
    slots = rows * n
    columns = grad_seq.shape[1]
    width = 512
    anywhere, vmem = pl.BlockSpec(memory_space=pltpu.HBM), pl.BlockSpec(memory_space=pltpu.VMEM)

    def kernel(*refs):
        fused_kernel(n, cuts, width, *refs)

    sums = 2 * (n - 1) * (len(cuts) - 1)
    return pl.pallas_call(
        kernel,
        out_shape=(jax.ShapeDtypeStruct((rows, hidden), jnp.float32),
                   jax.ShapeDtypeStruct((hidden, columns), jnp.float32),
                   jax.ShapeDtypeStruct((1, columns), jnp.float32)),
        in_specs=[anywhere, anywhere, anywhere, vmem],
        out_specs=(vmem, vmem, vmem),
        scratch_shapes=[
            pltpu.VMEM((slots, columns), jnp.bfloat16),
            pltpu.VMEM((hidden, columns), jnp.bfloat16),
            pltpu.VMEM((slots, hidden), jnp.bfloat16),
            pltpu.VMEM((rows, hidden), jnp.bfloat16),
            pltpu.VMEM((n, hidden, rows), jnp.bfloat16),
            pltpu.VMEM((hidden + 16, slots), jnp.bfloat16),
            pltpu.VMEM((rows, hidden), jnp.float32),
            pltpu.VMEM((slots, 128), jnp.int32),
            pltpu.VMEM((slots, 128), jnp.int32),
            pltpu.VMEM((rows, 128), jnp.int32),
            pltpu.VMEM((2, n - 1, rows, hidden), jnp.bfloat16),
            pltpu.VMEM((n - 1, rows, hidden), jnp.bfloat16),
            pltpu.SemaphoreType.DMA((14,)),
            pltpu.SemaphoreType.DMA((14,)),
            pltpu.SemaphoreType.DMA((2 * (n - 1),)),
            pltpu.SemaphoreType.DMA((2 * (n - 1),)),
            pltpu.SemaphoreType.DMA((sums,)),
            pltpu.SemaphoreType.DMA((sums,)),
            pltpu.SemaphoreType.DMA((4,)),
        ],
        compiler_params=pltpu.CompilerParams(
            collective_id=0, has_side_effects=True, vmem_limit_bytes=52 * 2**20),
    )(grad_seq, w_out, pre_act, places)


def arrival_order_fits(positions, n_tile, n_text, cuts):
    chip_rows = positions.shape[0] * 2 // n_text
    half = chip_rows // 4
    places = positions.reshape(1, n_tile, -1)
    chip = jnp.arange(n_text // 2, dtype=jnp.int32)[:, None, None]
    away = (places // chip_rows) ^ chip
    odd = places // half % 2
    soon = (away == 0) | (away == 1 + odd)
    later = away != 3
    counts = jnp.sum(soon.astype(jnp.int32) + later * 32768, axis=2)
    return jnp.all((counts % 32768 >= cuts[1]) & (counts // 32768 >= cuts[2]))


def line_sum(term, me, n, rows):
    def mine(block):
        start = jnp.clip(block, 0, n - 1) * rows
        return lax.dynamic_slice_in_dim(term, start, rows, 0).astype(jnp.float32)

    total = mine(me)
    right = left = None
    for step in range(1, n):
        ahead = n - step
        out_right, out_left = mine(me + ahead), mine(me - ahead)
        if right is not None:
            out_right = out_right + right.astype(jnp.float32)
            out_left = out_left + left.astype(jnp.float32)
        hops = range(min(step, n - 1))
        right = lax.ppermute(out_right.astype(jnp.bfloat16), "tile", [(i, i + 1) for i in hops])
        left = lax.ppermute(out_left.astype(jnp.bfloat16), "tile", [(n - 1 - i, n - 2 - i) for i in hops])
    return total + right.astype(jnp.float32) + left.astype(jnp.float32)


def solution(mesh):
    n_tile, n_text = mesh.shape["tile"], mesh.shape["text"]

    def steady(grad_seq, positions, pre_act, w_out):
        t, me = lax.axis_index("text"), lax.axis_index("tile")
        grows, columns = grad_seq.shape
        rows, hidden = pre_act.shape
        slots = positions.shape[0]
        around_text = [(i, (i + 1) % n_text) for i in range(n_text)]
        around_tile = [(i, (i + 1) % n_tile) for i in range(n_tile)]

        def places(tile):
            return lax.dynamic_slice_in_dim(positions, tile * rows, rows)

        def gather(k, carry):
            block, whole, term = carry
            block = jnp.where(k == 0, grad_seq, lax.ppermute(block, "text", around_text))
            start = (t - k) % n_text * grows
            part = jnp.einsum("so,ho->sh", block, w_out, preferred_element_type=jnp.float32)
            whole = lax.dynamic_update_slice_in_dim(whole, block, start, 0)
            term = lax.dynamic_update_slice_in_dim(term, part.astype(jnp.bfloat16), start, 0)
            return block, whole, term

        _, whole, term = lax.fori_loop(0, n_text, gather, (
            jnp.zeros_like(grad_seq), jnp.zeros((slots, columns), jnp.bfloat16), jnp.zeros((slots, hidden), jnp.bfloat16)))

        def activate(k, carry):
            block, act = carry
            block = jnp.where(k == 0, pre_act, lax.ppermute(block, "tile", around_tile))
            value = gelu_parts(block)[0].astype(jnp.bfloat16)
            act = act.at[places((me - k) % n_tile)].set(value, mode="promise_in_bounds", unique_indices=True)
            return block, act

        _, act = lax.fori_loop(0, n_tile, activate, (
            jnp.zeros_like(pre_act), jnp.zeros((slots, hidden), jnp.bfloat16)))

        def add(k, total):
            total = lax.ppermute(total, "tile", around_tile)
            return total + rows_of(term, places((me - 1 - k) % n_tile)).astype(jnp.float32)

        total = lax.fori_loop(0, n_tile, add, jnp.zeros((rows, hidden), jnp.float32))
        weight_term = jnp.einsum("sh,so->ho", act, whole, preferred_element_type=jnp.float32)
        return total * gelu_parts(pre_act)[1], weight_term, jnp.sum(whole, axis=0, dtype=jnp.float32)

    def plain(grad_seq, positions, pre_act, w_out):
        local_rows, hidden = pre_act.shape
        slots = positions.shape[0]
        me = lax.axis_index("tile")
        gathered = lax.all_gather(grad_seq, "text", axis=0, tiled=True)
        term = jnp.einsum(
            "so,ho->sh", gathered, w_out, preferred_element_type=jnp.float32).astype(jnp.bfloat16)

        blocks = [pre_act]
        for shift in range(1, n_tile):
            ring = [(i, (i + shift) % n_tile) for i in range(n_tile)]
            blocks.append(lax.ppermute(pre_act, "tile", ring))
        blocks = lax.optimization_barrier((blocks, term))[0]
        slot = jnp.arange(slots, dtype=jnp.int32)
        turned = (me - slot // local_rows) % n_tile * local_rows + slot % local_rows
        source = jnp.zeros((slots,), jnp.int32).at[positions].set(
            turned, mode="promise_in_bounds", unique_indices=True)
        act = jnp.concatenate([gelu_parts(b)[0].astype(jnp.bfloat16) for b in blocks], axis=0)
        act_seq = rows_of(act, source)
        slope = gelu_parts(pre_act)[1]

        cut = hidden // 2 // 128 * 128
        spans = [(0, cut), (cut, hidden)] if cut else [(0, hidden)]
        summed = []
        for lo, hi in spans:
            summed.append(line_sum(rows_of(term[:, lo:hi], positions), me, n_tile, local_rows))
        weight_term = jnp.einsum("sh,so->ho", act_seq, gathered, preferred_element_type=jnp.float32)
        local_sum = jnp.sum(gathered, axis=0, dtype=jnp.float32)
        grad_pre = jnp.concatenate(summed, axis=1) * slope
        return (grad_pre, weight_term, local_sum)

    def body(grad_seq, positions, pre_act, w_out):
        if n_tile != 4 or n_text != 8:
            return plain(grad_seq, positions, pre_act, w_out)
        rows = pre_act.shape[0]
        cuts = (0, rows * 2 // 5 // 16 * 16, rows * 27 // 40 // 16 * 16, rows)

        def quick(grad_seq, positions, pre_act, w_out):
            grad_pre, weight_term, bias = fused(n_tile, cuts, grad_seq, positions.reshape(-1, 128), pre_act, w_out)
            return (grad_pre, weight_term, bias.reshape(-1))

        fits = arrival_order_fits(positions, n_tile, n_text, cuts)
        args = (grad_seq, positions, pre_act, w_out)
        found = lax.while_loop(
            lambda carry: jnp.logical_not(carry[0]), lambda carry: (jnp.array(True), *steady(*args)),
            (fits, *quick(*args)))
        return found[1:]

    in_specs = (P("text", "tile"), P(), P("tile", "text"), P("text", "tile"))
    out_specs = (P("tile", "text"), P("text", "tile"), P("tile"))
    return jax.shard_map(body, mesh=mesh, in_specs=in_specs, out_specs=out_specs, check_vma=False)
```

```python
import jax
import jax.numpy as jnp
from jax import lax
from jax.experimental import pallas as pl
from jax.experimental.pallas import tpu as pltpu
from jax.sharding import PartitionSpec as P


def gelu_parts(pre):
    value = pre.astype(jnp.float32)
    cdf = 0.5 * (1.0 + jax.scipy.special.erf(value * 0.7071067811865476))
    activated = value * cdf
    slope = cdf + value * jnp.exp(-0.5 * value * value) * 0.3989422804014327
    return (activated, slope)


def rows_of(table, index):
    return table.at[index].get(mode="promise_in_bounds", unique_indices=True)


def fused_kernel(n, cuts, width, g_ref, w_ref, pre_ref, place_ref, grad_ref, weight_ref, bias_ref,
                 held, weight, term, pre, act, turned, own, spots, packs, ranks, arrive, leave,
                 send_sem, recv_sem, act_send, act_recv, sum_send, sum_recv, own_sem):
    t, me = lax.axis_index("text"), lax.axis_index("tile")
    core, x, y = t % 2, t // 2 % 2, t // 4
    across, beside, above = 1 - 2 * core, 2 - 4 * x, 4 - 8 * y
    mate, xn, yn = t + across, t + beside, t + above
    diag = t + beside + above
    mesh_ids = pl.DeviceIdType.MESH
    grows = g_ref.shape[0]
    half = grows // 2
    rows, hidden = pre_ref.shape
    slots, columns = held.shape
    lanes = 128
    groups = rows // lanes
    phases = len(cuts) - 1

    loads = [pltpu.make_async_copy(pre_ref, pre, own_sem.at[0]), pltpu.make_async_copy(w_ref, weight, own_sem.at[1])]
    for copy in loads:
        copy.start()
    barrier = pltpu.get_barrier_semaphore()
    for other in (mate, xn, yn):
        pl.semaphore_signal(barrier, inc=1, device_id={"text": other}, device_id_type=mesh_ids)
    for other in ((me + 1) % n, (me + n - 1) % n):
        pl.semaphore_signal(barrier, inc=1, device_id={"tile": other}, device_id_type=mesh_ids)
    pl.semaphore_wait(barrier, 5)

    def part(owner, k):
        return pl.ds(pl.multiple_of(owner * grows + k * half, 16), half)

    count = [0]

    def send(src, dst, other):
        k = count[0]
        count[0] += 1
        copy = pltpu.make_async_remote_copy(
            src_ref=src, dst_ref=held.at[dst], send_sem=send_sem.at[k], recv_sem=recv_sem.at[k],
            device_id={"text": other}, device_id_type=mesh_ids)
        copy.start()
        return copy

    def mine(k):
        return g_ref.at[pl.ds(k * half, half)]

    def pass_on(owner, k, other):
        return send(held.at[part(owner, k)], part(owner, k), other)

    def use(*parts):
        spans = [part(owner, k) for owner, k in parts]
        value = lax.dot_general(
            jnp.concatenate([held[at, :] for at in spans], axis=0), weight[...], (((1,), (1,)), ((), ())),
            preferred_element_type=jnp.float32).astype(term.dtype)
        for c, at in enumerate(spans):
            term[at, :] = value[c * half:(c + 1) * half]

    def place(way):
        return me if way == 0 else n - 1 - me

    def act_copy(way, step, block):
        k = way * (n - 1) + step - 1
        return pltpu.make_async_remote_copy(
            src_ref=act.at[block], dst_ref=act.at[block], send_sem=act_send.at[k], recv_sem=act_recv.at[k],
            device_id={"tile": me + 1 - 2 * way}, device_id_type=mesh_ids)

    def act_hop(way, step):
        return act_copy(way, step, me - step + 1 if way == 0 else me + step - 1)

    def act_come(way, step):
        return act_copy(way, step, me - step if way == 0 else me + step)

    def act_next(step):
        for way in range(2):
            i = place(way)

            @pl.when(i >= step)
            def _():
                act_come(way, step).wait_recv()

                @pl.when(i < n - 1)
                def _():
                    act_hop(way, step + 1).start()

    def reorder(block, first):
        def run(c, carry):
            start = pl.multiple_of(c * width, width)
            column = lax.broadcasted_iota(jnp.int32, (rows, width), 1) + start
            at = pl.ds(pl.multiple_of(block * rows, lanes), rows)
            pick = jnp.where(column == spots[at, :][:, :1], 1.0, 0.0).astype(jnp.bfloat16)
            moved = jnp.dot(act[block], pick, preferred_element_type=jnp.float32)
            to = (pl.ds(0, hidden), pl.ds(start, width))
            if not first:
                moved = moved + turned[to].astype(jnp.float32)
            turned[to] = moved.astype(jnp.bfloat16)
            return carry

        lax.fori_loop(0, slots // width, run, 0)

    def reorder_come(step):
        def run(way, carry):
            i = me + way * (n - 1 - 2 * me)

            @pl.when(i >= step)
            def _():
                reorder(me - step + 2 * step * way, False)
            return carry

        lax.fori_loop(0, 2, run, 0)

    x0 = send(mine(0), part(t, 0), xn)
    y0 = send(mine(1), part(t, 1), yn)
    x1 = send(mine(1), part(t, 1), xn)
    y1 = send(mine(0), part(t, 0), yn)
    m0 = send(mine(0), part(t, 0), mate)
    m1 = send(mine(1), part(t, 1), mate)
    keep = [pltpu.make_async_copy(mine(k), held.at[part(t, k)], own_sem.at[2 + k]) for k in range(2)]
    for copy in keep:
        copy.start()

    loads[0].wait()

    def activate(c, carry):
        at = pl.ds(pl.multiple_of(c * lanes, lanes), lanes)
        activated, slope = gelu_parts(pre[at, :])
        grad_ref[at, :] = slope
        act[me, :, at] = activated.T.astype(jnp.bfloat16)
        return carry

    lax.fori_loop(0, groups, activate, 0)
    for way in range(2):
        @pl.when(place(way) < n - 1)
        def _():
            act_hop(way, 1).start()

    def clear(c, carry):
        term[pl.ds(pl.multiple_of(c * half, 16), half), :] = jnp.zeros((half, hidden), jnp.bfloat16)
        return carry

    lax.fori_loop(0, slots // half, clear, 0)
    turned[pl.ds(hidden, 16), :] = jnp.ones((16, slots), jnp.bfloat16)

    loads[1].wait()
    for k in range(2):
        keep[k].wait()

    def column_of(row):
        return jnp.broadcast_to(row, (lanes, lanes)).T

    earlier = jnp.where(
        lax.broadcasted_iota(jnp.int32, (rows, rows), 0) < lax.broadcasted_iota(jnp.int32, (rows, rows), 1),
        1.0, 0.0).astype(jnp.bfloat16)

    def rank_tile(d, carry):
        pieces = [place_ref[pl.ds(d * groups + g, 1), :] for g in range(groups)]
        row = jnp.concatenate(pieces, axis=1)

        def among(start, size):
            return jnp.where((row >= start) & (row < start + size), 1.0, 0.0)

        soon = among((t - core) * grows, 2 * grows)
        for owner, k in ((xn, 0), (yn, 1)):
            soon = soon + among(owner * grows + k * half, half) + among((owner + across) * grows + k * half, half)
        later = (among((xn - core) * grows, 2 * grows) + among((yn - core) * grows, 2 * grows)
                 + among((t - core) * grows, 2 * grows) - soon)
        late = 1.0 - soon - later
        kinds = jnp.concatenate([soon, later, late, jnp.zeros((13, rows), jnp.float32)], axis=0)
        before = jnp.dot(kinds.astype(jnp.bfloat16), earlier, preferred_element_type=jnp.float32)
        n_soon = jnp.sum(soon, axis=1, keepdims=True)
        n_later = jnp.sum(later, axis=1, keepdims=True)
        rank = (soon * before[0:1] + later * (before[1:2] + n_soon)
                + late * (before[2:3] + n_soon + n_later)).astype(jnp.int32)
        high = row >> 6
        parts = jnp.concatenate([high, row - (high << 6), jnp.zeros((14, rows), jnp.int32)], axis=0)
        parts = parts.astype(jnp.float32).astype(jnp.bfloat16)
        spread = lax.broadcasted_iota(jnp.int32, (lanes, rows), 1)
        total = jnp.zeros((16, rows), jnp.float32)
        for g in range(groups):
            span = slice(g * lanes, (g + 1) * lanes)
            column = column_of(rank[:, span])

            @pl.when(d == me)
            def _():
                ranks[span, :] = column
            pick = jnp.where(spread == column[:, :1], 1.0, 0.0).astype(jnp.bfloat16)
            total = total + jnp.dot(parts[:, span], pick, preferred_element_type=jnp.float32)
        packed = (total[0:1] * 64.0 + total[1:2]).astype(jnp.int32)
        for g in range(groups):
            span = slice(g * lanes, (g + 1) * lanes)
            at = pl.ds(pl.multiple_of(d * rows + g * lanes, lanes), lanes)
            packs[at, :] = column_of(packed[:, span])
            spots[at, :] = column_of(pieces[g])
        return carry

    lax.fori_loop(0, n, rank_tile, 0)

    is_end = (me == 0) | (me == n - 1)
    toward = jnp.where(me * 2 < n, 0, 1)

    def chosen(table, starts, size):
        spans = [pl.ds(pl.multiple_of(start, 16), size) for start in starts]
        column = lax.broadcasted_iota(jnp.int32, (size, slots), 1)
        picks = [jnp.where(column == table[at, :][:, :1], 1.0, 0.0).astype(jnp.bfloat16) for at in spans]
        pick = jnp.concatenate(picks, axis=0) if len(picks) > 1 else picks[0]
        return jnp.dot(pick, term[...], preferred_element_type=jnp.float32)

    def pick_sums(phase):
        size = cuts[phase + 1] - cuts[phase]
        tiles = []
        for slot in range(n - 1):
            first = (1 - toward) * (n - 1 - slot) + toward * slot
            tiles.append(first if slot < n - 2 else jnp.where(is_end, first, toward * (n - 1)))
        value = chosen(packs, [tile * rows + cuts[phase] for tile in tiles], size).astype(jnp.bfloat16)
        for slot in range(n - 1):
            leave[slot, pl.ds(cuts[phase], size), :] = value[slot * size:(slot + 1) * size]

    def hop(way, step, phase, slot):
        piece = pl.ds(cuts[phase], cuts[phase + 1] - cuts[phase])
        k = (way * (n - 1) + step - 1) * phases + phase
        return pltpu.make_async_remote_copy(
            src_ref=leave.at[slot, piece], dst_ref=arrive.at[way, step - 1, piece],
            send_sem=sum_send.at[k], recv_sem=sum_recv.at[k],
            device_id={"tile": me + 1 - 2 * way}, device_id_type=mesh_ids)

    def sum_step(phase, i, way, step):
        size = cuts[phase + 1] - cuts[phase]
        piece = pl.ds(cuts[phase], size)
        slot = step - 1 if i < 2 else i
        if i:
            hop(way, step, phase, slot).wait_recv()
            value = (leave[slot, piece, :].astype(jnp.float32)
                     + arrive[way, step - 1, piece, :].astype(jnp.float32))
            leave[slot, piece, :] = value.astype(jnp.bfloat16)
        hop(way, step, phase, slot).start()

    def sums(phase, i):
        way = toward if i < 2 else 1 - toward

        def run(step, carry):
            sum_step(phase, i, way, step)
            return carry

        lax.fori_loop(1, n - i, run, 0)

    def ends(phase):
        @pl.when(is_end)
        def _():
            sums(phase, 0)

    def middle(phase, i):
        @pl.when(jnp.logical_not(is_end))
        def _():
            sums(phase, i)

    from_left = jnp.minimum(n - me, n - 1)
    from_right = jnp.minimum(me + 1, n - 1)

    def collect(phase):
        size = cuts[phase + 1] - cuts[phase]
        column = lax.broadcasted_iota(jnp.int32, (rows, size), 1) + cuts[phase]
        for way, there, step in ((0, me > 0, from_left), (1, me < n - 1, from_right)):
            @pl.when(there)
            def _():
                hop(way, step, phase, 0).wait_recv()

                back = jnp.where(column == ranks[:, :1], 1.0, 0.0).astype(jnp.bfloat16)
                own[...] += jnp.dot(
                    back, arrive[way, step - 1, pl.ds(cuts[phase], size), :], preferred_element_type=jnp.float32)

    def weigh(first, upto):
        def run(c, carry):
            at = pl.ds(pl.multiple_of(c * width, width), width)
            both = jnp.dot(turned[...], held[:, at], preferred_element_type=jnp.float32)
            weight_ref[:, at] = both[:hidden]
            bias_ref[:, at] = both[hidden:hidden + 1]
            return carry

        lax.fori_loop(first, upto, run, 0)

    m0.wait_recv()
    m1.wait_recv()
    use((t, 0), (t, 1), (mate, 0), (mate, 1))

    x0.wait_recv()
    yf = pass_on(xn, 0, yn)
    mx0 = pass_on(xn, 0, mate)
    y0.wait_recv()
    xf = pass_on(yn, 1, xn)
    my0 = pass_on(yn, 1, mate)
    mx0.wait_recv()
    my0.wait_recv()
    use((xn, 0), (yn, 1), (xn + across, 0), (yn + across, 1))
    pick_sums(0)
    ends(0)

    reorder(me, True)
    act_next(1)
    reorder_come(1)

    x1.wait_recv()
    mx1 = pass_on(xn, 1, mate)
    y1.wait_recv()
    my1 = pass_on(yn, 0, mate)
    mx1.wait_recv()
    my1.wait_recv()
    use((xn, 1), (yn, 0), (xn + across, 1), (yn + across, 0))
    pick_sums(1)
    ends(1)
    middle(0, 1)
    act_next(2)
    reorder_come(2)

    yf.wait_recv()
    md0 = pass_on(diag, 0, mate)
    xf.wait_recv()
    md1 = pass_on(diag, 1, mate)
    md0.wait_recv()
    md1.wait_recv()
    use((diag, 0), (diag, 1), (diag + across, 0), (diag + across, 1))
    pick_sums(2)
    ends(2)
    middle(0, 2)
    middle(1, 1)
    own[...] = chosen(spots, [me * rows], rows)
    middle(1, 2)
    act_next(3)
    reorder_come(3)
    blocks = columns // width
    weigh(0, blocks // 4)
    middle(2, 1)
    weigh(blocks // 4, blocks // 2)
    middle(2, 2)
    collect(0)
    collect(1)
    weigh(blocks // 2, blocks)
    collect(2)

    def finish(c, carry):
        at = pl.ds(pl.multiple_of(c * lanes, lanes), lanes)
        grad_ref[at, :] = own[at, :] * grad_ref[at, :]
        return carry

    lax.fori_loop(0, groups, finish, 0)

    for copy in (x0, y0, x1, y1, m0, m1, yf, mx0, xf, my0, mx1, my1, md0, md1):
        copy.wait_send()
    for way in range(2):
        for step in range(1, n):
            @pl.when((place(way) >= step - 1) & (place(way) < n - 1))
            def _():
                act_hop(way, step).wait_send()

            @pl.when(place(way) < n - step)
            def _():
                for phase in range(phases):
                    hop(way, step, phase, 0).wait_send()


def fused(n, cuts, grad_seq, places, pre_act, w_out):
    rows, hidden = pre_act.shape
    slots = rows * n
    columns = grad_seq.shape[1]
    width = 512
    anywhere, vmem = pl.BlockSpec(memory_space=pltpu.HBM), pl.BlockSpec(memory_space=pltpu.VMEM)

    def kernel(*refs):
        fused_kernel(n, cuts, width, *refs)

    sums = 2 * (n - 1) * (len(cuts) - 1)
    return pl.pallas_call(
        kernel,
        out_shape=(pltpu.VMEM((rows, hidden), jnp.float32),
                   pltpu.VMEM((hidden, columns), jnp.float32),
                   pltpu.VMEM((1, columns), jnp.float32)),
        in_specs=[anywhere, anywhere, anywhere, vmem],
        out_specs=(vmem, vmem, vmem),
        scratch_shapes=[
            pltpu.VMEM((slots, columns), jnp.bfloat16),
            pltpu.VMEM((hidden, columns), jnp.bfloat16),
            pltpu.VMEM((slots, hidden), jnp.bfloat16),
            pltpu.VMEM((rows, hidden), jnp.bfloat16),
            pltpu.VMEM((n, hidden, rows), jnp.bfloat16),
            pltpu.VMEM((hidden + 16, slots), jnp.bfloat16),
            pltpu.VMEM((rows, hidden), jnp.float32),
            pltpu.VMEM((slots, 128), jnp.int32),
            pltpu.VMEM((slots, 128), jnp.int32),
            pltpu.VMEM((rows, 128), jnp.int32),
            pltpu.VMEM((2, n - 1, rows, hidden), jnp.bfloat16),
            pltpu.VMEM((n - 1, rows, hidden), jnp.bfloat16),
            pltpu.SemaphoreType.DMA((14,)),
            pltpu.SemaphoreType.DMA((14,)),
            pltpu.SemaphoreType.DMA((2 * (n - 1),)),
            pltpu.SemaphoreType.DMA((2 * (n - 1),)),
            pltpu.SemaphoreType.DMA((sums,)),
            pltpu.SemaphoreType.DMA((sums,)),
            pltpu.SemaphoreType.DMA((4,)),
        ],
        compiler_params=pltpu.CompilerParams(
            collective_id=0, has_side_effects=True, vmem_limit_bytes=52 * 2**20),
    )(grad_seq, w_out, pre_act, places)


def arrival_order_fits(positions, n_tile, n_text, cuts):
    chip_rows = positions.shape[0] * 2 // n_text
    half = chip_rows // 4
    places = positions.reshape(1, n_tile, -1)
    chip = jnp.arange(n_text // 2, dtype=jnp.int32)[:, None, None]
    away = (places // chip_rows) ^ chip
    odd = places // half % 2
    soon = (away == 0) | (away == 1 + odd)
    later = away != 3
    counts = jnp.sum(soon.astype(jnp.int32) + later * 32768, axis=2)
    return jnp.all((counts % 32768 >= cuts[1]) & (counts // 32768 >= cuts[2]))


def line_sum(term, me, n, rows):
    def mine(block):
        start = jnp.clip(block, 0, n - 1) * rows
        return lax.dynamic_slice_in_dim(term, start, rows, 0).astype(jnp.float32)

    total = mine(me)
    right = left = None
    for step in range(1, n):
        ahead = n - step
        out_right, out_left = mine(me + ahead), mine(me - ahead)
        if right is not None:
            out_right = out_right + right.astype(jnp.float32)
            out_left = out_left + left.astype(jnp.float32)
        hops = range(min(step, n - 1))
        right = lax.ppermute(out_right.astype(jnp.bfloat16), "tile", [(i, i + 1) for i in hops])
        left = lax.ppermute(out_left.astype(jnp.bfloat16), "tile", [(n - 1 - i, n - 2 - i) for i in hops])
    return total + right.astype(jnp.float32) + left.astype(jnp.float32)


def solution(mesh):
    n_tile, n_text = mesh.shape["tile"], mesh.shape["text"]

    def steady(grad_seq, positions, pre_act, w_out):
        t, me = lax.axis_index("text"), lax.axis_index("tile")
        grows, columns = grad_seq.shape
        rows, hidden = pre_act.shape
        slots = positions.shape[0]
        around_text = [(i, (i + 1) % n_text) for i in range(n_text)]
        around_tile = [(i, (i + 1) % n_tile) for i in range(n_tile)]

        def places(tile):
            return lax.dynamic_slice_in_dim(positions, tile * rows, rows)

        def gather(k, carry):
            block, whole, term = carry
            block = jnp.where(k == 0, grad_seq, lax.ppermute(block, "text", around_text))
            start = (t - k) % n_text * grows
            part = jnp.einsum("so,ho->sh", block, w_out, preferred_element_type=jnp.float32)
            whole = lax.dynamic_update_slice_in_dim(whole, block, start, 0)
            term = lax.dynamic_update_slice_in_dim(term, part.astype(jnp.bfloat16), start, 0)
            return block, whole, term

        _, whole, term = lax.fori_loop(0, n_text, gather, (
            jnp.zeros_like(grad_seq), jnp.zeros((slots, columns), jnp.bfloat16), jnp.zeros((slots, hidden), jnp.bfloat16)))

        def activate(k, carry):
            block, act = carry
            block = jnp.where(k == 0, pre_act, lax.ppermute(block, "tile", around_tile))
            value = gelu_parts(block)[0].astype(jnp.bfloat16)
            act = act.at[places((me - k) % n_tile)].set(value, mode="promise_in_bounds", unique_indices=True)
            return block, act

        _, act = lax.fori_loop(0, n_tile, activate, (
            jnp.zeros_like(pre_act), jnp.zeros((slots, hidden), jnp.bfloat16)))

        def add(k, total):
            total = lax.ppermute(total, "tile", around_tile)
            return total + rows_of(term, places((me - 1 - k) % n_tile)).astype(jnp.float32)

        total = lax.fori_loop(0, n_tile, add, jnp.zeros((rows, hidden), jnp.float32))
        weight_term = jnp.einsum("sh,so->ho", act, whole, preferred_element_type=jnp.float32)
        return total * gelu_parts(pre_act)[1], weight_term, jnp.sum(whole, axis=0, dtype=jnp.float32)

    def plain(grad_seq, positions, pre_act, w_out):
        local_rows, hidden = pre_act.shape
        slots = positions.shape[0]
        me = lax.axis_index("tile")
        gathered = lax.all_gather(grad_seq, "text", axis=0, tiled=True)
        term = jnp.einsum(
            "so,ho->sh", gathered, w_out, preferred_element_type=jnp.float32).astype(jnp.bfloat16)

        blocks = [pre_act]
        for shift in range(1, n_tile):
            ring = [(i, (i + shift) % n_tile) for i in range(n_tile)]
            blocks.append(lax.ppermute(pre_act, "tile", ring))
        blocks = lax.optimization_barrier((blocks, term))[0]
        slot = jnp.arange(slots, dtype=jnp.int32)
        turned = (me - slot // local_rows) % n_tile * local_rows + slot % local_rows
        source = jnp.zeros((slots,), jnp.int32).at[positions].set(
            turned, mode="promise_in_bounds", unique_indices=True)
        act = jnp.concatenate([gelu_parts(b)[0].astype(jnp.bfloat16) for b in blocks], axis=0)
        act_seq = rows_of(act, source)
        slope = gelu_parts(pre_act)[1]

        cut = hidden // 2 // 128 * 128
        spans = [(0, cut), (cut, hidden)] if cut else [(0, hidden)]
        summed = []
        for lo, hi in spans:
            summed.append(line_sum(rows_of(term[:, lo:hi], positions), me, n_tile, local_rows))
        weight_term = jnp.einsum("sh,so->ho", act_seq, gathered, preferred_element_type=jnp.float32)
        local_sum = jnp.sum(gathered, axis=0, dtype=jnp.float32)
        grad_pre = jnp.concatenate(summed, axis=1) * slope
        return (grad_pre, weight_term, local_sum)

    def body(grad_seq, positions, pre_act, w_out):
        if n_tile != 4 or n_text != 8:
            return plain(grad_seq, positions, pre_act, w_out)
        rows = pre_act.shape[0]
        cuts = (0, rows * 2 // 5 // 16 * 16, rows * 27 // 40 // 16 * 16, rows)

        def quick(grad_seq, positions, pre_act, w_out):
            grad_pre, weight_term, bias = fused(n_tile, cuts, grad_seq, positions.reshape(-1, 128), pre_act, w_out)
            return (grad_pre, weight_term, bias.reshape(-1))

        fits = arrival_order_fits(positions, n_tile, n_text, cuts)
        args = (grad_seq, positions, pre_act, w_out)
        first = [jnp.where(fits, value, 0.0) for value in quick(*args)]
        found = lax.while_loop(
            lambda carry: jnp.logical_not(carry[0]), lambda carry: (jnp.array(True), *steady(*args)),
            (fits, *first))
        return found[1:]

    in_specs = (P("text", "tile"), P(), P("tile", "text"), P("text", "tile"))
    out_specs = (P("tile", "text"), P("text", "tile"), P("tile"))
    return jax.shard_map(body, mesh=mesh, in_specs=in_specs, out_specs=out_specs, check_vma=False)
```
